128 devices in a mesh: ctx: 16 (over x, z), ch: 8 (over y, core).
Axes of the slice: x: 4, y: 4, z: 4, core: 2. Of those that a mesh axis runs over, the one named last changes fastest.
Arguments:
- grad_out: float32 [16, 524288], P('ch', 'ctx'), may hold values from -6 to 6
- gate_in: float32 [16, 524288], P('ch', 'ctx'), may hold values from -6 to 6
- input_spectrum: float32 [2, 16, 32, 32768], P(None, 'ch', 'ctx'), may hold values from -6 to 6
- filter_spectrum: float32 [2, 4, 32, 32768], P(None, None, 'ctx'), may hold values from -6 to 6
Outputs:
- grad_input: float32 [16, 524288], P('ch', 'ctx')
- grad_gate: float32 [16, 524288], P('ch', 'ctx')
- grad_filter: float32 [4, 524288], P(None, 'ctx')
The draws below stay inside these ranges and needn't reach their ends.
All inputs are finite; a program needn't handle non-finite values.
Results may differ from the reference program's by a relative error of at most 0.0003.
Values sent between devices are 32-bit elements; how exact they have to be, the bound alone decides.
A program may use at most 192 MiB of HBM per device.

```python
import jax
import jax.numpy as jnp
from jax import lax

CHANNELS = 16
FILTERS = 4
RADIX = 32
COLS = 32768
LENGTH = 524288


def steps_of(rng, extent, cuts, smallest, top_value):
    def one(position, shards_of):
        draws = jax.random.uniform(jax.random.fold_in(jax.random.fold_in(rng, 6), position), (shards_of,), jnp.float32, smallest / len(cuts), top_value / len(cuts))
        return jnp.repeat(jnp.exp(draws), extent[position] // shards_of).reshape((-1,) + (1,) * (len(extent) - position - 1))

    gain = one(*cuts[0])
    for cut in cuts[1:]:
        gain = gain * one(*cut)
    return gain


def normal_values(own_key, shape, scale, limit, cuts=(), held_as=jnp.bfloat16):
    values = scale * jax.random.normal(own_key, shape, jnp.float32)
    if cuts:
        values = values * steps_of(own_key, shape, cuts, -0.22, 0.18)
    return jnp.clip(values, -limit, limit).astype(held_as)


def setup_inputs(seed: int = 0) -> dict:
    streams_of = jax.random.split(jax.random.key(seed), 5)
    grad_out = normal_values(streams_of[0], (CHANNELS, LENGTH), 1.0, 6.0, ((0, 8), (1, 16)), jnp.float32)
    gate_in = normal_values(streams_of[1], (CHANNELS, LENGTH), 1.0, 6.0, ((0, 8), (1, 16)), jnp.float32)
    input_spectrum = normal_values(streams_of[2], (2, CHANNELS, RADIX, COLS), 1.0, 6.0, ((1, 8), (2, 16)), jnp.float32)
    filter_spectrum = normal_values(streams_of[3], (2, FILTERS, RADIX, COLS), 1.0, 6.0, ((2, 16),), jnp.float32)
    return dict(grad_out=grad_out, gate_in=gate_in, input_spectrum=input_spectrum, filter_spectrum=filter_spectrum)


def natural(spectrum):
    flat = jnp.transpose(spectrum, (0, 2, 1)).reshape(2, RADIX * COLS)
    return lax.complex(flat[0], flat[1])


def inverse_head(values):
    return jnp.real(jnp.fft.ifft(values, norm="ortho"))[:LENGTH]


def channel_terms(inputs, filter_spectrum):
    grad_row, gate_row, in_spectrum, channel_index = inputs
    gated_grad = grad_row * gate_row
    padded = jnp.concatenate([gated_grad, jnp.zeros_like(gated_grad)])
    gated_spec = jnp.fft.fft(padded, norm="ortho")
    filt = lax.dynamic_index_in_dim(filter_spectrum, channel_index // (CHANNELS // FILTERS), axis=1, keepdims=False)
    in_nat = natural(in_spectrum)
    filt_nat = natural(filt)
    conv = inverse_head(in_nat * filt_nat)
    grad_in = inverse_head(jnp.conj(filt_nat) * gated_spec)
    grad_filt = inverse_head(jnp.conj(in_nat) * gated_spec)
    return grad_in, grad_row * conv, grad_filt


def reference(grad_out, gate_in, input_spectrum, filter_spectrum):
    per_channel = jnp.moveaxis(input_spectrum, 1, 0)
    indices = jnp.arange(CHANNELS, dtype=jnp.int32)
    grad_input, grad_gate, filter_terms = lax.map(
        lambda inputs: channel_terms(inputs, filter_spectrum),
        (grad_out, gate_in, per_channel, indices))
    grad_filter = filter_terms.reshape(FILTERS, CHANNELS // FILTERS, LENGTH).sum(1)
    return grad_input, grad_gate, grad_filter
```

```python
from functools import partial
import math

import jax
import jax.numpy as jnp
import numpy as np
from jax import lax
from jax.experimental import pallas as pl
from jax.experimental.pallas import tpu as pltpu
from jax.sharding import PartitionSpec as P

CHANNELS = 16
FILTERS = 4
RADIX = 32
COLS = 32768
TOTAL = RADIX * COLS
SHARDS = 16
WIDE = 256
LANES = 128
MESH = pl.DeviceIdType.MESH
F32 = jnp.float32
BF16 = jnp.bfloat16


def real_form(matrix):
    return np.block([[matrix.real, -matrix.imag], [matrix.imag, matrix.real]])


def halves(matrix):
    whole = matrix.astype(np.float32)
    high = whole.astype(jnp.bfloat16)
    low = (matrix - high.astype(np.float64)).astype(np.float32).astype(jnp.bfloat16)
    return np.stack([high, low])


def tables():
    def unit(counts, modulus):
        return np.exp(-2j * np.pi * (counts % modulus) / modulus)

    wide = np.arange(WIDE)
    lanes = np.arange(LANES)
    rows = np.arange(RADIX)
    dft_wide = unit(wide[:, None] * wide[None, :], WIDE)
    dft_lanes = unit(lanes[:, None] * lanes[None, :], LANES)
    inner = unit(wide[:, None] * lanes[None, :], COLS) * 2.0**-10
    lane_rows = unit(rows[:, None] * lanes[None, :], TOTAL)
    wide_rows = unit(wide[:, None] * rows[None, :], TOTAL // LANES)
    picked = np.concatenate([wide_rows.real, wide_rows.imag, np.zeros((WIDE, LANES - 2 * RADIX))], axis=1)
    return (
        np.stack([halves(real_form(dft_wide)), halves(real_form(dft_wide.conj()))]),
        np.stack([halves(real_form(dft_lanes)), halves(real_form(dft_lanes.conj()))]),
        np.stack([inner.real, inner.imag]).astype(np.float32),
        np.stack([lane_rows.real, lane_rows.imag]).astype(np.float32),
        picked.astype(np.float32),
    )


def times_unit(value, turn):
    re, im = value
    turn = turn % 1.0
    if turn == 0.0:
        return re, im
    if turn == 0.5:
        return negated(re), negated(im)
    if turn == 0.25:
        return negated(im), re
    if turn == 0.75:
        return im, negated(re)
    c, s = math.cos(2 * math.pi * turn), math.sin(2 * math.pi * turn)
    if im is None:
        return re * c, re * s
    if re is None:
        return im * (-s), im * c
    if turn in (0.125, 0.375, 0.625, 0.875):
        h = math.sqrt(0.5)
        if turn == 0.125:
            return (re - im) * h, (re + im) * h
        if turn == 0.375:
            return (re + im) * (-h), (re - im) * h
        if turn == 0.625:
            return (im - re) * h, (re + im) * (-h)
        return (re + im) * h, (im - re) * h
    return re * c - im * s, re * s + im * c


def negated(x):
    return None if x is None else -x


def plus(a, b):
    if a is None:
        return b
    return a if b is None else a + b


def minus(a, b):
    if b is None:
        return a
    return -b if a is None else a - b


def real_dft(xs):
    n = len(xs)
    if n == 1:
        return [(xs[0], None)]
    even, odd = real_dft(xs[0::2]), real_dft(xs[1::2])
    if n == 2:
        a, b = even[0][0], odd[0][0]
        return [(plus(a, b), None), (minus(a, b), None)]
    out = [None] * (n // 2 + 1)
    for k in range(n // 4 + 1):
        e, t = even[k], times_unit(odd[k], -k / n)
        out[k] = (plus(e[0], t[0]), plus(e[1], t[1]))
        if n // 2 - k != k:
            out[n // 2 - k] = (minus(e[0], t[0]), minus(t[1], e[1]))
    return out


def back_dft(xs, first_half=False):
    n = len(xs)
    if n == 1:
        return list(xs)
    even, odd = back_dft(xs[0::2]), back_dft(xs[1::2])
    upper, lower = [], []
    for k in range(n // 2):
        e, t = even[k], times_unit(odd[k], k / n)
        upper.append((e[0] + t[0], e[1] + t[1]))
        if not first_half:
            lower.append((e[0] - t[0], e[1] - t[1]))
    return upper + lower


def parts(x):
    high = x.astype(BF16)
    return high, (x - high.astype(F32)).astype(BF16)


def product(left, x, nt=False):
    high, low = parts(x)
    dims = (((1,), (1 if nt else 0,)), ((), ()))
    dot = partial(lax.dot_general, dimension_numbers=dims, preferred_element_type=F32)
    return dot(left[0], high) + (dot(left[0], low) + dot(left[1], high))


def kernel(
    grad_hbm, gate_hbm, spec_hbm, filt_hbm, wide_hbm, lanes_hbm, inner_hbm, lane_rows_hbm, picked_hbm,
    gi_hbm, gg_hbm, gf_hbm,
    grad, gate, spec, filt, wide, lanes, inner, lane_rows, picked,
    pre, mid, midt,
    x_out, x_in, y_out, y_in, c_out, c_in, i_out, i_in, d_out, d_in, e_out, e_in,
    prods, fsum, fpart, f_out, f_in, g_out, g_in, g_all, gf,
    load_sem, send_sem, recv_sem,
):
    me = lax.axis_index("ctx")
    group = lax.axis_index("ch")
    core = group % 2
    plane = group // 2
    other = group + 1 - 2 * core

    def load(k, src, dst):
        copy = pltpu.make_async_copy(src, dst, load_sem.at[k])
        copy.start()
        return copy

    loads = [
        load(0, grad_hbm, grad),
        load(1, gate_hbm, gate),
        load(2, inner_hbm, inner),
        load(3, lane_rows_hbm, lane_rows),
        load(4, picked_hbm, picked),
        load(5, spec_hbm, spec),
        load(6, filt_hbm.at[:, plane], filt),
        load(7, lanes_hbm, lanes),
        load(8, wide_hbm, wide),
    ]

    barrier = pltpu.get_barrier_semaphore()
    pl.semaphore_signal(barrier, inc=1, device_id={"ch": other}, device_id_type=MESH)
    for step in range(1, SHARDS):
        peer = (me + step) % SHARDS
        pl.semaphore_signal(barrier, inc=1, device_id={"ctx": peer}, device_id_type=MESH)
        pl.semaphore_signal(barrier, inc=1, device_id={"ctx": peer, "ch": other}, device_id_type=MESH)
    for step in range(1, 4):
        for side in range(2):
            there = 2 * ((plane + step) % 4) + side
            pl.semaphore_signal(barrier, inc=1, device_id={"ch": there}, device_id_type=MESH)
    pl.semaphore_wait(barrier, 2 * SHARDS - 1 + 6)

    def send_all(k, out, into):
        for step in range(1, SHARDS):
            peer = (me + step) % SHARDS
            pltpu.make_async_remote_copy(
                out.at[peer], into.at[me], send_sem.at[k], recv_sem.at[k],
                device_id={"ctx": peer}, device_id_type=MESH,
            ).start()
        into[me] = out[me]

    def bulk(k, ref):
        return pltpu.make_async_remote_copy(
            ref, ref, send_sem.at[k], recv_sem.at[k], device_id={"ctx": (me + 1) % SHARDS}, device_id_type=MESH
        )

    def arrived(k, into):
        bulk(k, into.at[pl.ds(0, SHARDS - 1)]).wait_recv()

    def left(k, out):
        bulk(k, out.at[pl.ds(0, SHARDS - 1)]).wait_send()

    loads[0].wait()
    loads[1].wait()
    x_out[...] = (grad[...] * gate[...]).reshape(SHARDS, 32, LANES)
    send_all(0, x_out, x_in)

    for k in (2, 3, 4):
        loads[k].wait()
    lane_ids = lax.broadcasted_iota(jnp.int32, (WIDE, LANES), 1)
    for b in range(2):
        row = 2 * me + b
        for ri in range(2):
            column = jnp.sum(jnp.where(lane_ids == row + RADIX * ri, picked[...], 0.0), axis=1, keepdims=True)
            pre[b, ri] = jnp.broadcast_to(column, (WIDE, LANES))
        vr = lane_rows[0, pl.ds(row, 1), :]
        vi = lane_rows[1, pl.ds(row, 1), :]
        tr = inner[0] * vr - inner[1] * vi
        ti = inner[0] * vi + inner[1] * vr
        mid[b, 0] = tr
        mid[b, 1] = ti
        midt[b, 0] = tr.T * 0.5
        midt[b, 1] = ti.T * 0.5

    for k in (5, 6, 7, 8):
        loads[k].wait()

    def spread(ref, b):
        return jnp.concatenate([ref[pl.ds(2 * s + b, LANES, stride=4), :] for s in range(2)], axis=1)

    def inverse_rows(b, arrays):
        mr, mi = midt[b, 0], midt[b, 1]
        stacked = []
        for re, im in arrays:
            c = product(lanes[1], jnp.concatenate([re, im], axis=0))
            cr, ci = c[:LANES], c[LANES:]
            stacked.append(jnp.concatenate([cr * mr + ci * mi, ci * mr - cr * mi], axis=1))
        t = product(wide[1], jnp.concatenate(stacked, axis=0) if len(stacked) > 1 else stacked[0], nt=True)
        pr, pi = pre[b, 0], pre[b, 1]
        out = []
        for k in range(len(arrays)):
            sr = t[:WIDE, LANES * k : LANES * (k + 1)]
            si = t[WIDE:, LANES * k : LANES * (k + 1)]
            out.append((sr * pr + si * pi, si * pr - sr * pi))
        return out

    def fill(out, b, arrays):
        for ch, (re, im) in enumerate(inverse_rows(b, arrays)):
            out[:, b, 0, ch] = re.reshape(SHARDS, 16, LANES)
            out[:, b, 1, ch] = im.reshape(SHARDS, 16, LANES)

    for b in range(2):
        hr, hi = spread(filt.at[0], b), spread(filt.at[1], b)
        prods[b, 0, 0], prods[b, 0, 1] = hr, hi
        for ch in range(2):
            ur, ui = spread(spec.at[0, ch], b), spread(spec.at[1, ch], b)
            prods[b, 1 + ch, 0], prods[b, 1 + ch, 1] = ur, ui

    def conv_row(b, carry):
        hr, hi = prods[b, 0, 0], prods[b, 0, 1]
        arrays = []
        for ch in range(2):
            ur, ui = prods[b, 1 + ch, 0], prods[b, 1 + ch, 1]
            arrays.append((ur * hr - ui * hi, ur * hi + ui * hr))
        fill(c_out, b, arrays)
        return carry

    arrived(0, x_in)

    def slab_forward(step, carry):
        ch, half = step // 2, step % 2
        xs = [x_in[j, pl.ds(16 * half + ch, 8, stride=2), :] for j in range(SHARDS)]
        ys = real_dft(xs + [None] * SHARDS)
        at = pl.ds(pl.multiple_of(8 * half, 8), 8)
        for r in range(RADIX):
            re, im = ys[min(r, RADIX - r)]
            if im is None:
                im = jnp.zeros_like(re)
            elif r > RADIX // 2:
                im = -im
            y_out[r // 2, r % 2, 0, ch, at, :] = re
            y_out[r // 2, r % 2, 1, ch, at, :] = im
        return carry

    lax.fori_loop(0, 4, slab_forward, 0)
    send_all(1, y_out, y_in)

    lax.fori_loop(0, 2, conv_row, 0)
    send_all(2, c_out, c_in)

    arrived(1, y_in)

    def forward_row(b, carry):
        pr = jnp.concatenate([pre[b, 0]] * 2, axis=1)
        pi = jnp.concatenate([pre[b, 1]] * 2, axis=1)
        yr = jnp.concatenate([y_in[:, b, 0, ch].reshape(WIDE, LANES) for ch in range(2)], axis=1)
        yi = jnp.concatenate([y_in[:, b, 1, ch].reshape(WIDE, LANES) for ch in range(2)], axis=1)
        a = product(wide[0], jnp.concatenate([yr * pr - yi * pi, yr * pi + yi * pr], axis=0))
        mr, mi = mid[b, 0], mid[b, 1]
        fr = fi = None
        for ch in range(2):
            ar = a[:WIDE, LANES * ch : LANES * (ch + 1)]
            ai = a[WIDE:, LANES * ch : LANES * (ch + 1)]
            g = product(lanes[0], jnp.concatenate([ar * mr - ai * mi, ar * mi + ai * mr], axis=1), nt=True)
            gr, gi = g[:LANES], g[LANES:]
            ur, ui = prods[b, 1 + ch, 0], prods[b, 1 + ch, 1]
            wr, wi = ur * gr + ui * gi, ur * gi - ui * gr
            fr, fi = (wr, wi) if ch == 0 else (fr + wr, fi + wi)
            hr, hi = prods[b, 0, 0], prods[b, 0, 1]
            prods[b, 1 + ch, 0], prods[b, 1 + ch, 1] = hr * gr + hi * gi, hr * gi - hi * gr
        fsum[b, 0], fsum[b, 1] = fr, fi
        return carry

    lax.fori_loop(0, 2, forward_row, 0)

    swap = pltpu.make_async_remote_copy(
        fsum.at[1 - core], fpart, send_sem.at[3], recv_sem.at[3], device_id={"ch": other}, device_id_type=MESH
    )
    swap.start()

    def input_row(b, carry):
        fill(i_out, b, [(prods[b, 1 + ch, 0], prods[b, 1 + ch, 1]) for ch in range(2)])
        return carry

    swap.wait_recv()
    ((re, im),) = inverse_rows(core, [(fsum[core, 0] + fpart[0], fsum[core, 1] + fpart[1])])
    f_out[:, 0] = re.reshape(2 * SHARDS, 8, LANES)
    f_out[:, 1] = im.reshape(2 * SHARDS, 8, LANES)
    for step in range(SHARDS):
        peer = (me + step) % SHARDS
        for side in range(2):
            if step == 0 and side == 0:
                continue
            there = other if side else group
            half = 1 - core if side else core
            pltpu.make_async_remote_copy(
                f_out.at[2 * peer + half], f_in.at[2 * me + core], send_sem.at[4], recv_sem.at[4],
                device_id={"ctx": peer, "ch": there}, device_id_type=MESH,
            ).start()
    f_in[2 * me + core] = f_out[2 * me + core]

    lax.fori_loop(0, 2, input_row, 0)
    send_all(5, i_out, i_in)

    def slab_back(src, out):
        def body(half, carry):
            at = pl.ds(pl.multiple_of(8 * half, 8), 8)

            def row(r, ri, ch):
                return src[r // 2, r % 2, ri, ch, at, :]

            ws = [None] * RADIX
            for r in range(RADIX // 2 + 1):
                q = (RADIX - r) % RADIX
                a = row(r, 0, 0) + row(q, 0, 0)
                c = row(r, 0, 1) + row(q, 0, 1)
                if q == r:
                    ws[r] = (a, c)
                    continue
                bb = row(r, 1, 0) - row(q, 1, 0)
                d = row(r, 1, 1) - row(q, 1, 1)
                ws[r] = (a - d, bb + c)
                ws[q] = (a + d, c - bb)
            for j, (re, im) in enumerate(back_dft(ws, first_half=True)):
                out[j, pl.ds(16 * half, 8, stride=2), :] = re
                out[j, pl.ds(16 * half + 1, 8, stride=2), :] = im
            return carry

        lax.fori_loop(0, 2, body, 0)

    arrived(2, c_in)
    slab_back(c_in, d_out)
    send_all(6, d_out, d_in)

    bulk(4, f_in.at[pl.ds(0, 2 * SHARDS - 1)]).wait_recv()
    ws = [(f_in[r, 0], f_in[r, 1]) for r in range(RADIX)]
    for j, (re, _) in enumerate(back_dft(ws, first_half=True)):
        g_out[j] = re + re
    send_all(7, g_out, g_in)

    arrived(5, i_in)
    slab_back(i_in, e_out)
    send_all(8, e_out, e_in)

    arrived(7, g_in)
    for step in range(4):
        for side in range(2):
            if step == 0 and side == 0:
                continue
            there = 2 * ((plane + step) % 4) + (1 - core if side else core)
            pltpu.make_async_remote_copy(
                g_in, g_all.at[group], send_sem.at[9], recv_sem.at[9],
                device_id={"ch": there}, device_id_type=MESH,
            ).start()
    g_all[group] = g_in[...]

    arrived(6, d_in)
    gate[...] = grad[...] * d_in[...].reshape(512, LANES)
    store_gg = load(1, gate, gg_hbm)
    arrived(8, e_in)
    store_gi = load(0, e_in, gi_hbm)
    bulk(9, g_all.at[pl.ds(0, 7)]).wait_recv()
    for f in range(FILTERS):
        for c in range(2):
            for q in range(SHARDS):
                gf[pl.ds(64 * q + 32 * c + f, 8, stride=4), :] = g_all[2 * f + c, q]
    store_gf = load(2, gf, gf_hbm)

    left(0, x_out)
    left(1, y_out)
    left(2, c_out)
    swap.wait_send()
    bulk(4, f_out.at[pl.ds(0, 2 * SHARDS - 1)]).wait_send()
    left(5, i_out)
    left(6, d_out)
    left(7, g_out)
    left(8, e_out)
    bulk(9, g_all.at[pl.ds(0, 7)]).wait_send()
    store_gg.wait()
    store_gi.wait()
    store_gf.wait()


def per_device(grad_out, gate_in, input_spectrum, filter_spectrum):
    def tiled(x):
        lead = x.shape[:-2]
        pieces = x.reshape(*lead, x.shape[-2], WIDE, LANES)
        return jnp.swapaxes(pieces, -3, -2).reshape(*lead, WIDE * x.shape[-2], LANES)

    def untiled(x, rows):
        return jnp.swapaxes(x.reshape(WIDE, rows, LANES), 0, 1).reshape(rows, COLS)

    consts = tables()
    operands = (tiled(grad_out), tiled(gate_in), tiled(input_spectrum), tiled(filter_spectrum), *consts)
    slab = lambda *dims: pltpu.VMEM((SHARDS, *dims, LANES), F32)
    wave = slab(2, 2, 2, 16)
    scratch = [
        pltpu.VMEM((512, LANES), F32),
        pltpu.VMEM((512, LANES), F32),
        pltpu.VMEM((2, 2, 512, LANES), F32),
        pltpu.VMEM((2, 512, LANES), F32),
        *[pltpu.VMEM(c.shape, c.dtype) for c in consts],
        pltpu.VMEM((2, 2, WIDE, LANES), F32),
        pltpu.VMEM((2, 2, WIDE, LANES), F32),
        pltpu.VMEM((2, 2, LANES, WIDE), F32),
        slab(32),
        slab(32),
        wave,
        wave,
        wave,
        wave,
        wave,
        wave,
        slab(32),
        slab(32),
        slab(32),
        slab(32),
        pltpu.VMEM((2, 3, 2, LANES, WIDE), F32),
        pltpu.VMEM((2, 2, LANES, WIDE), F32),
        pltpu.VMEM((2, LANES, WIDE), F32),
        pltpu.VMEM((2 * SHARDS, 2, 8, LANES), F32),
        pltpu.VMEM((2 * SHARDS, 2, 8, LANES), F32),
        slab(8),
        slab(8),
        pltpu.VMEM((8, SHARDS, 8, LANES), F32),
        pltpu.VMEM((1024, LANES), F32),
        pltpu.SemaphoreType.DMA((9,)),
        pltpu.SemaphoreType.DMA((10,)),
        pltpu.SemaphoreType.DMA((10,)),
    ]
    anywhere = pl.BlockSpec(memory_space=pl.ANY)
    grad_input, grad_gate, grad_filter = pl.pallas_call(
        kernel,
        out_shape=[
            jax.ShapeDtypeStruct((SHARDS, 32, LANES), F32),
            jax.ShapeDtypeStruct((512, LANES), F32),
            jax.ShapeDtypeStruct((1024, LANES), F32),
        ],
        in_specs=[anywhere] * len(operands),
        out_specs=[anywhere] * 3,
        scratch_shapes=scratch,
        compiler_params=pltpu.CompilerParams(
            collective_id=0, has_side_effects=True, vmem_limit_bytes=40 * 2**20
        ),
        name="gated_conv_back",
    )(*operands)
    return (
        untiled(grad_input.reshape(512, LANES), 2),
        untiled(grad_gate, 2),
        untiled(grad_filter, 4),
    )


def solution(mesh):
    return jax.shard_map(
        per_device,
        mesh=mesh,
        in_specs=(
            P("ch", "ctx"),
            P("ch", "ctx"),
            P(None, "ch", "ctx", None),
            P(None, None, "ctx", None),
        ),
        out_specs=(P("ch", "ctx"), P("ch", "ctx"), P(None, "ctx")),
        check_vma=False,
    )
```

```python
from functools import partial
import math

import jax
import jax.numpy as jnp
import numpy as np
from jax import lax
from jax.experimental import pallas as pl
from jax.experimental.pallas import tpu as pltpu
from jax.sharding import PartitionSpec as P

CHANNELS = 16
FILTERS = 4
RADIX = 32
COLS = 32768
TOTAL = RADIX * COLS
SHARDS = 16
WIDE = 256
LANES = 128
MESH = pl.DeviceIdType.MESH
STEPS = (
    (2, 2), (2, 1), (1, 2), (2, 3), (3, 2), (2, 0), (0, 2),
    (1, 1), (3, 3), (1, 3), (3, 1), (1, 0), (0, 1), (3, 0), (0, 3),
)
F32 = jnp.float32
BF16 = jnp.bfloat16


def real_form(matrix):
    return np.block([[matrix.real, -matrix.imag], [matrix.imag, matrix.real]])


def halves(matrix):
    whole = matrix.astype(np.float32)
    high = whole.astype(jnp.bfloat16)
    low = (matrix - high.astype(np.float64)).astype(np.float32).astype(jnp.bfloat16)
    return np.stack([high, low])


def tables():
    def unit(counts, modulus):
        return np.exp(-2j * np.pi * (counts % modulus) / modulus)

    wide = np.arange(WIDE)
    lanes = np.arange(LANES)
    rows = np.arange(RADIX)
    dft_wide = unit(wide[:, None] * wide[None, :], WIDE)
    dft_lanes = unit(lanes[:, None] * lanes[None, :], LANES)
    inner = unit(wide[:, None] * lanes[None, :], COLS) * 2.0**-10
    lane_rows = unit(rows[:, None] * lanes[None, :], TOTAL)
    wide_rows = unit(wide[:, None] * rows[None, :], TOTAL // LANES)
    picked = np.concatenate([wide_rows.real, wide_rows.imag, np.zeros((WIDE, LANES - 2 * RADIX))], axis=1)
    return (
        np.stack([halves(real_form(dft_wide)), halves(real_form(dft_wide.conj()))]),
        np.stack([halves(real_form(dft_lanes)), halves(real_form(dft_lanes.conj()))]),
        np.stack([inner.real, inner.imag]).astype(np.float32),
        np.stack([lane_rows.real, lane_rows.imag]).astype(np.float32),
        picked.astype(np.float32),
    )


def times_unit(value, turn):
    re, im = value
    turn = turn % 1.0
    if turn == 0.0:
        return re, im
    if turn == 0.5:
        return negated(re), negated(im)
    if turn == 0.25:
        return negated(im), re
    if turn == 0.75:
        return im, negated(re)
    c, s = math.cos(2 * math.pi * turn), math.sin(2 * math.pi * turn)
    if im is None:
        return re * c, re * s
    if re is None:
        return im * (-s), im * c
    if turn in (0.125, 0.375, 0.625, 0.875):
        h = math.sqrt(0.5)
        if turn == 0.125:
            return (re - im) * h, (re + im) * h
        if turn == 0.375:
            return (re + im) * (-h), (re - im) * h
        if turn == 0.625:
            return (im - re) * h, (re + im) * (-h)
        return (re + im) * h, (im - re) * h
    return re * c - im * s, re * s + im * c


def negated(x):
    return None if x is None else -x


def plus(a, b):
    if a is None:
        return b
    return a if b is None else a + b


def minus(a, b):
    if b is None:
        return a
    return -b if a is None else a - b


def real_dft(xs):
    n = len(xs)
    if n == 1:
        return [(xs[0], None)]
    even, odd = real_dft(xs[0::2]), real_dft(xs[1::2])
    if n == 2:
        a, b = even[0][0], odd[0][0]
        return [(plus(a, b), None), (minus(a, b), None)]
    out = [None] * (n // 2 + 1)
    for k in range(n // 4 + 1):
        e, t = even[k], times_unit(odd[k], -k / n)
        out[k] = (plus(e[0], t[0]), plus(e[1], t[1]))
        if n // 2 - k != k:
            out[n // 2 - k] = (minus(e[0], t[0]), minus(t[1], e[1]))
    return out


def back_dft(xs, first_half=False):
    n = len(xs)
    if n == 1:
        return list(xs)
    even, odd = back_dft(xs[0::2]), back_dft(xs[1::2])
    upper, lower = [], []
    for k in range(n // 2):
        e, t = even[k], times_unit(odd[k], k / n)
        upper.append((e[0] + t[0], e[1] + t[1]))
        if not first_half:
            lower.append((e[0] - t[0], e[1] - t[1]))
    return upper + lower


def parts(x):
    high = x.astype(BF16)
    return high, (x - high.astype(F32)).astype(BF16)


def product(left, x, nt=False):
    high, low = parts(x)
    dims = (((1,), (1 if nt else 0,)), ((), ()))
    dot = partial(lax.dot_general, dimension_numbers=dims, preferred_element_type=F32)
    return dot(left[0], high) + (dot(left[0], low) + dot(left[1], high))


def kernel(
    grad_hbm, gate_hbm, spec_hbm, filt_hbm, wide_hbm, lanes_hbm, inner_hbm, lane_rows_hbm, picked_hbm,
    gi_hbm, gg_hbm, gf_hbm,
    grad, gate, spec, filt, wide, lanes, inner, lane_rows, picked,
    pre, mid, midt,
    x_out, x_in, y_out, y_in, c_out, c_in, i_out, i_in, d_out, d_in, e_out, e_in,
    prods, fsum, fpart, f_out, f_in, g_out, g_in, g_all, gf,
    load_sem, send_sem, recv_sem,
):
    me = lax.axis_index("ctx")
    group = lax.axis_index("ch")
    core = group % 2
    plane = group // 2
    other = group + 1 - 2 * core
    peers = [(me // 4 + dx) % 4 * 4 + (me + dz) % 4 for dx, dz in STEPS]

    def load(k, src, dst):
        copy = pltpu.make_async_copy(src, dst, load_sem.at[k])
        copy.start()
        return copy

    loads = [
        load(0, grad_hbm, grad),
        load(1, gate_hbm, gate),
        load(2, inner_hbm, inner),
        load(3, lane_rows_hbm, lane_rows),
        load(4, picked_hbm, picked),
        load(5, spec_hbm, spec),
        load(6, filt_hbm.at[:, plane], filt),
        load(7, lanes_hbm, lanes),
        load(8, wide_hbm, wide),
    ]

    barrier = pltpu.get_barrier_semaphore()
    pl.semaphore_signal(barrier, inc=1, device_id={"ch": other}, device_id_type=MESH)
    for peer in peers:
        pl.semaphore_signal(barrier, inc=1, device_id={"ctx": peer}, device_id_type=MESH)
        pl.semaphore_signal(barrier, inc=1, device_id={"ctx": peer, "ch": other}, device_id_type=MESH)
    for step in range(1, 4):
        for side in range(2):
            there = 2 * ((plane + step) % 4) + side
            pl.semaphore_signal(barrier, inc=1, device_id={"ch": there}, device_id_type=MESH)
    pl.semaphore_wait(barrier, 2 * SHARDS - 1 + 6)

    def send_all(k, out, into):
        for peer in peers:
            pltpu.make_async_remote_copy(
                out.at[peer], into.at[me], send_sem.at[k], recv_sem.at[k],
                device_id={"ctx": peer}, device_id_type=MESH,
            ).start()
        into[me] = out[me]

    def bulk(k, ref):
        return pltpu.make_async_remote_copy(
            ref, ref, send_sem.at[k], recv_sem.at[k], device_id={"ctx": (me + 1) % SHARDS}, device_id_type=MESH
        )

    def arrived(k, into):
        bulk(k, into.at[pl.ds(0, SHARDS - 1)]).wait_recv()

    def left(k, out):
        bulk(k, out.at[pl.ds(0, SHARDS - 1)]).wait_send()

    loads[0].wait()
    loads[1].wait()
    x_out[...] = (grad[...] * gate[...]).reshape(SHARDS, 32, LANES)
    send_all(0, x_out, x_in)

    for k in (2, 3, 4):
        loads[k].wait()
    lane_ids = lax.broadcasted_iota(jnp.int32, (WIDE, LANES), 1)
    for b in range(2):
        row = 2 * me + b
        for ri in range(2):
            column = jnp.sum(jnp.where(lane_ids == row + RADIX * ri, picked[...], 0.0), axis=1, keepdims=True)
            pre[b, ri] = jnp.broadcast_to(column, (WIDE, LANES))
        vr = lane_rows[0, pl.ds(row, 1), :]
        vi = lane_rows[1, pl.ds(row, 1), :]
        tr = inner[0] * vr - inner[1] * vi
        ti = inner[0] * vi + inner[1] * vr
        mid[b, 0] = tr
        mid[b, 1] = ti
        midt[b, 0] = tr.T * 0.5
        midt[b, 1] = ti.T * 0.5

    for k in (5, 6, 7, 8):
        loads[k].wait()

    def spread(ref, b):
        return jnp.concatenate([ref[pl.ds(2 * s + b, LANES, stride=4), :] for s in range(2)], axis=1)

    def inverse_rows(b, arrays):
        mr, mi = midt[b, 0], midt[b, 1]
        stacked = []
        for re, im in arrays:
            c = product(lanes[1], jnp.concatenate([re, im], axis=0))
            cr, ci = c[:LANES], c[LANES:]
            stacked.append(jnp.concatenate([cr * mr + ci * mi, ci * mr - cr * mi], axis=1))
        t = product(wide[1], jnp.concatenate(stacked, axis=0) if len(stacked) > 1 else stacked[0], nt=True)
        pr, pi = pre[b, 0], pre[b, 1]
        out = []
        for k in range(len(arrays)):
            sr = t[:WIDE, LANES * k : LANES * (k + 1)]
            si = t[WIDE:, LANES * k : LANES * (k + 1)]
            out.append((sr * pr + si * pi, si * pr - sr * pi))
        return out

    def fill(out, b, arrays):
        for ch, (re, im) in enumerate(inverse_rows(b, arrays)):
            out[:, b, 0, ch] = re.reshape(SHARDS, 16, LANES)
            out[:, b, 1, ch] = im.reshape(SHARDS, 16, LANES)

    for b in range(2):
        hr, hi = spread(filt.at[0], b), spread(filt.at[1], b)
        prods[b, 0, 0], prods[b, 0, 1] = hr, hi
        for ch in range(2):
            ur, ui = spread(spec.at[0, ch], b), spread(spec.at[1, ch], b)
            prods[b, 1 + ch, 0], prods[b, 1 + ch, 1] = ur, ui

    def conv_row(b, carry):
        hr, hi = prods[b, 0, 0], prods[b, 0, 1]
        arrays = []
        for ch in range(2):
            ur, ui = prods[b, 1 + ch, 0], prods[b, 1 + ch, 1]
            arrays.append((ur * hr - ui * hi, ur * hi + ui * hr))
        fill(c_out, b, arrays)
        return carry

    arrived(0, x_in)

    def slab_forward(step, carry):
        ch, half = step // 2, step % 2
        xs = [x_in[j, pl.ds(16 * half + ch, 8, stride=2), :] for j in range(SHARDS)]
        ys = real_dft(xs + [None] * SHARDS)
        at = pl.ds(pl.multiple_of(8 * half, 8), 8)
        for r in range(RADIX):
            re, im = ys[min(r, RADIX - r)]
            if im is None:
                im = jnp.zeros_like(re)
            elif r > RADIX // 2:
                im = -im
            y_out[r // 2, r % 2, 0, ch, at, :] = re
            y_out[r // 2, r % 2, 1, ch, at, :] = im
        return carry

    lax.fori_loop(0, 4, slab_forward, 0)
    send_all(1, y_out, y_in)

    lax.fori_loop(0, 2, conv_row, 0)
    send_all(2, c_out, c_in)

    arrived(1, y_in)

    def forward_row(b, carry):
        pr = jnp.concatenate([pre[b, 0]] * 2, axis=1)
        pi = jnp.concatenate([pre[b, 1]] * 2, axis=1)
        yr = jnp.concatenate([y_in[:, b, 0, ch].reshape(WIDE, LANES) for ch in range(2)], axis=1)
        yi = jnp.concatenate([y_in[:, b, 1, ch].reshape(WIDE, LANES) for ch in range(2)], axis=1)
        a = product(wide[0], jnp.concatenate([yr * pr - yi * pi, yr * pi + yi * pr], axis=0))
        mr, mi = mid[b, 0], mid[b, 1]
        fr = fi = None
        for ch in range(2):
            ar = a[:WIDE, LANES * ch : LANES * (ch + 1)]
            ai = a[WIDE:, LANES * ch : LANES * (ch + 1)]
            g = product(lanes[0], jnp.concatenate([ar * mr - ai * mi, ar * mi + ai * mr], axis=1), nt=True)
            gr, gi = g[:LANES], g[LANES:]
            ur, ui = prods[b, 1 + ch, 0], prods[b, 1 + ch, 1]
            wr, wi = ur * gr + ui * gi, ur * gi - ui * gr
            fr, fi = (wr, wi) if ch == 0 else (fr + wr, fi + wi)
            hr, hi = prods[b, 0, 0], prods[b, 0, 1]
            prods[b, 1 + ch, 0], prods[b, 1 + ch, 1] = hr * gr + hi * gi, hr * gi - hi * gr
        fsum[b, 0], fsum[b, 1] = fr, fi
        return carry

    lax.fori_loop(0, 2, forward_row, 0)

    swap = pltpu.make_async_remote_copy(
        fsum.at[1 - core], fpart, send_sem.at[3], recv_sem.at[3], device_id={"ch": other}, device_id_type=MESH
    )
    swap.start()

    def input_row(b, carry):
        fill(i_out, b, [(prods[b, 1 + ch, 0], prods[b, 1 + ch, 1]) for ch in range(2)])
        return carry

    swap.wait_recv()
    ((re, im),) = inverse_rows(core, [(fsum[core, 0] + fpart[0], fsum[core, 1] + fpart[1])])
    f_out[:, 0] = re.reshape(2 * SHARDS, 8, LANES)
    f_out[:, 1] = im.reshape(2 * SHARDS, 8, LANES)
    for peer in peers + [me]:
        for side in range(2):
            if peer is me and side == 0:
                continue
            there = other if side else group
            half = 1 - core if side else core
            pltpu.make_async_remote_copy(
                f_out.at[2 * peer + half], f_in.at[2 * me + core], send_sem.at[4], recv_sem.at[4],
                device_id={"ctx": peer, "ch": there}, device_id_type=MESH,
            ).start()
    f_in[2 * me + core] = f_out[2 * me + core]

    lax.fori_loop(0, 2, input_row, 0)
    send_all(5, i_out, i_in)

    def slab_back(src, out):
        def body(half, carry):
            at = pl.ds(pl.multiple_of(8 * half, 8), 8)

            def row(r, ri, ch):
                return src[r // 2, r % 2, ri, ch, at, :]

            ws = [None] * RADIX
            for r in range(RADIX // 2 + 1):
                q = (RADIX - r) % RADIX
                a = row(r, 0, 0) + row(q, 0, 0)
                c = row(r, 0, 1) + row(q, 0, 1)
                if q == r:
                    ws[r] = (a, c)
                    continue
                bb = row(r, 1, 0) - row(q, 1, 0)
                d = row(r, 1, 1) - row(q, 1, 1)
                ws[r] = (a - d, bb + c)
                ws[q] = (a + d, c - bb)
            for j, (re, im) in enumerate(back_dft(ws, first_half=True)):
                out[j, pl.ds(16 * half, 8, stride=2), :] = re
                out[j, pl.ds(16 * half + 1, 8, stride=2), :] = im
            return carry

        lax.fori_loop(0, 2, body, 0)

    arrived(2, c_in)
    slab_back(c_in, d_out)
    send_all(6, d_out, d_in)

    bulk(4, f_in.at[pl.ds(0, 2 * SHARDS - 1)]).wait_recv()
    ws = [(f_in[r, 0], f_in[r, 1]) for r in range(RADIX)]
    for j, (re, _) in enumerate(back_dft(ws, first_half=True)):
        g_out[j] = re + re
    send_all(7, g_out, g_in)

    arrived(5, i_in)
    slab_back(i_in, e_out)
    send_all(8, e_out, e_in)

    arrived(7, g_in)
    for step in range(4):
        for side in range(2):
            if step == 0 and side == 0:
                continue
            there = 2 * ((plane + step) % 4) + (1 - core if side else core)
            pltpu.make_async_remote_copy(
                g_in, g_all.at[group], send_sem.at[9], recv_sem.at[9],
                device_id={"ch": there}, device_id_type=MESH,
            ).start()
    g_all[group] = g_in[...]

    arrived(6, d_in)
    gate[...] = grad[...] * d_in[...].reshape(512, LANES)
    store_gg = load(1, gate, gg_hbm)
    arrived(8, e_in)
    store_gi = load(0, e_in, gi_hbm)
    bulk(9, g_all.at[pl.ds(0, 7)]).wait_recv()
    for f in range(FILTERS):
        for c in range(2):
            for q in range(SHARDS):
                gf[pl.ds(64 * q + 32 * c + f, 8, stride=4), :] = g_all[2 * f + c, q]
    store_gf = load(2, gf, gf_hbm)

    left(0, x_out)
    left(1, y_out)
    left(2, c_out)
    swap.wait_send()
    bulk(4, f_out.at[pl.ds(0, 2 * SHARDS - 1)]).wait_send()
    left(5, i_out)
    left(6, d_out)
    left(7, g_out)
    left(8, e_out)
    bulk(9, g_all.at[pl.ds(0, 7)]).wait_send()
    store_gg.wait()
    store_gi.wait()
    store_gf.wait()


def per_device(grad_out, gate_in, input_spectrum, filter_spectrum):
    def tiled(x):
        lead = x.shape[:-2]
        pieces = x.reshape(*lead, x.shape[-2], WIDE, LANES)
        return jnp.swapaxes(pieces, -3, -2).reshape(*lead, WIDE * x.shape[-2], LANES)

    def untiled(x, rows):
        return jnp.swapaxes(x.reshape(WIDE, rows, LANES), 0, 1).reshape(rows, COLS)

    consts = tables()
    operands = (tiled(grad_out), tiled(gate_in), tiled(input_spectrum), tiled(filter_spectrum), *consts)
    slab = lambda *dims: pltpu.VMEM((SHARDS, *dims, LANES), F32)
    wave = slab(2, 2, 2, 16)
    scratch = [
        pltpu.VMEM((512, LANES), F32),
        pltpu.VMEM((512, LANES), F32),
        pltpu.VMEM((2, 2, 512, LANES), F32),
        pltpu.VMEM((2, 512, LANES), F32),
        *[pltpu.VMEM(c.shape, c.dtype) for c in consts],
        pltpu.VMEM((2, 2, WIDE, LANES), F32),
        pltpu.VMEM((2, 2, WIDE, LANES), F32),
        pltpu.VMEM((2, 2, LANES, WIDE), F32),
        slab(32),
        slab(32),
        wave,
        wave,
        wave,
        wave,
        wave,
        wave,
        slab(32),
        slab(32),
        slab(32),
        slab(32),
        pltpu.VMEM((2, 3, 2, LANES, WIDE), F32),
        pltpu.VMEM((2, 2, LANES, WIDE), F32),
        pltpu.VMEM((2, LANES, WIDE), F32),
        pltpu.VMEM((2 * SHARDS, 2, 8, LANES), F32),
        pltpu.VMEM((2 * SHARDS, 2, 8, LANES), F32),
        slab(8),
        slab(8),
        pltpu.VMEM((8, SHARDS, 8, LANES), F32),
        pltpu.VMEM((1024, LANES), F32),
        pltpu.SemaphoreType.DMA((9,)),
        pltpu.SemaphoreType.DMA((10,)),
        pltpu.SemaphoreType.DMA((10,)),
    ]
    anywhere = pl.BlockSpec(memory_space=pltpu.HBM)
    grad_input, grad_gate, grad_filter = pl.pallas_call(
        kernel,
        out_shape=[
            jax.ShapeDtypeStruct((SHARDS, 32, LANES), F32),
            jax.ShapeDtypeStruct((512, LANES), F32),
            jax.ShapeDtypeStruct((1024, LANES), F32),
        ],
        in_specs=[anywhere] * len(operands),
        out_specs=[anywhere] * 3,
        scratch_shapes=scratch,
        compiler_params=pltpu.CompilerParams(
            collective_id=0, has_side_effects=True, vmem_limit_bytes=60 * 2**20
        ),
        name="gated_conv_back",
    )(*operands)
    return (
        untiled(grad_input.reshape(512, LANES), 2),
        untiled(grad_gate, 2),
        untiled(grad_filter, 4),
    )


def solution(mesh):
    return jax.shard_map(
        per_device,
        mesh=mesh,
        in_specs=(
            P("ch", "ctx"),
            P("ch", "ctx"),
            P(None, "ch", "ctx", None),
            P(None, None, "ctx", None),
        ),
        out_specs=(P("ch", "ctx"), P("ch", "ctx"), P(None, "ctx")),
        check_vma=False,
    )
```

```python
from functools import partial
import math

import jax
import jax.numpy as jnp
import numpy as np
from jax import lax
from jax.experimental import pallas as pl
from jax.experimental.pallas import tpu as pltpu
from jax.sharding import PartitionSpec as P

CHANNELS = 16
FILTERS = 4
RADIX = 32
COLS = 32768
TOTAL = RADIX * COLS
SHARDS = 16
WIDE = 256
LANES = 128
MESH = pl.DeviceIdType.MESH
STEPS = (
    (2, 2), (2, 1), (1, 2), (2, 3), (3, 2), (2, 0), (0, 2),
    (1, 1), (3, 3), (1, 3), (3, 1), (1, 0), (0, 1), (3, 0), (0, 3),
)
F32 = jnp.float32
BF16 = jnp.bfloat16


def real_form(matrix):
    return np.block([[matrix.real, -matrix.imag], [matrix.imag, matrix.real]])


def halves(matrix):
    whole = matrix.astype(np.float32)
    high = whole.astype(jnp.bfloat16)
    low = (matrix - high.astype(np.float64)).astype(np.float32).astype(jnp.bfloat16)
    return np.stack([high, low])


def tables():
    def unit(counts, modulus):
        return np.exp(-2j * np.pi * (counts % modulus) / modulus)

    wide = np.arange(WIDE)
    lanes = np.arange(LANES)
    rows = np.arange(RADIX)
    dft_wide = unit(wide[:, None] * wide[None, :], WIDE)
    dft_lanes = unit(lanes[:, None] * lanes[None, :], LANES)
    inner = unit(wide[:, None] * lanes[None, :], COLS) * 2.0**-10
    lane_rows = unit(rows[:, None] * lanes[None, :], TOTAL)
    wide_rows = unit(wide[:, None] * rows[None, :], TOTAL // LANES)
    picked = np.concatenate([wide_rows.real, wide_rows.imag, np.zeros((WIDE, LANES - 2 * RADIX))], axis=1)
    return (
        np.stack([halves(real_form(dft_wide)), halves(real_form(dft_wide.conj()))]),
        np.stack([halves(real_form(dft_lanes)), halves(real_form(dft_lanes.conj()))]),
        np.stack([inner.real, inner.imag]).astype(np.float32),
        np.stack([lane_rows.real, lane_rows.imag]).astype(np.float32),
        picked.astype(np.float32),
    )


def times_unit(value, turn):
    re, im = value
    turn = turn % 1.0
    if turn == 0.0:
        return re, im
    if turn == 0.5:
        return negated(re), negated(im)
    if turn == 0.25:
        return negated(im), re
    if turn == 0.75:
        return im, negated(re)
    c, s = math.cos(2 * math.pi * turn), math.sin(2 * math.pi * turn)
    if im is None:
        return re * c, re * s
    if re is None:
        return im * (-s), im * c
    if turn in (0.125, 0.375, 0.625, 0.875):
        h = math.sqrt(0.5)
        if turn == 0.125:
            return (re - im) * h, (re + im) * h
        if turn == 0.375:
            return (re + im) * (-h), (re - im) * h
        if turn == 0.625:
            return (im - re) * h, (re + im) * (-h)
        return (re + im) * h, (im - re) * h
    return re * c - im * s, re * s + im * c


def negated(x):
    return None if x is None else -x


def plus(a, b):
    if a is None:
        return b
    return a if b is None else a + b


def minus(a, b):
    if b is None:
        return a
    return -b if a is None else a - b


def real_dft(xs):
    n = len(xs)
    if n == 1:
        return [(xs[0], None)]
    even, odd = real_dft(xs[0::2]), real_dft(xs[1::2])
    if n == 2:
        a, b = even[0][0], odd[0][0]
        return [(plus(a, b), None), (minus(a, b), None)]
    out = [None] * (n // 2 + 1)
    for k in range(n // 4 + 1):
        e, t = even[k], times_unit(odd[k], -k / n)
        out[k] = (plus(e[0], t[0]), plus(e[1], t[1]))
        if n // 2 - k != k:
            out[n // 2 - k] = (minus(e[0], t[0]), minus(t[1], e[1]))
    return out


def back_dft(xs, first_half=False):
    n = len(xs)
    if n == 1:
        return list(xs)
    even, odd = back_dft(xs[0::2]), back_dft(xs[1::2])
    upper, lower = [], []
    for k in range(n // 2):
        e, t = even[k], times_unit(odd[k], k / n)
        upper.append((e[0] + t[0], e[1] + t[1]))
        if not first_half:
            lower.append((e[0] - t[0], e[1] - t[1]))
    return upper + lower


def parts(x):
    high = x.astype(BF16)
    return high, (x - high.astype(F32)).astype(BF16)


def product(left, x, nt=False):
    high, low = parts(x)
    dims = (((1,), (1 if nt else 0,)), ((), ()))
    dot = partial(lax.dot_general, dimension_numbers=dims, preferred_element_type=F32)
    return dot(left[0], high) + (dot(left[0], low) + dot(left[1], high))


def kernel(
    grad_hbm, gate_hbm, spec_hbm, filt_hbm, wide_hbm, lanes_hbm, inner_hbm, lane_rows_hbm, picked_hbm,
    gi_out, gg_out, gf_out,
    grad, gate, spec, filt, wide, lanes, inner, lane_rows, picked,
    pre, mid, midt,
    x_out, x_in, y_out, y_in, c_out, c_in, i_out, i_in, d_out, d_in, e_out, e_in,
    prods, fsum, fpart, f_out, f_in, g_out, g_in, g_all, gf,
    load_sem, send_sem, recv_sem,
):
    me = lax.axis_index("ctx")
    group = lax.axis_index("ch")
    core = group % 2
    plane = group // 2
    other = group + 1 - 2 * core
    peers = [(me // 4 + dx) % 4 * 4 + (me + dz) % 4 for dx, dz in STEPS]

    def load(k, src, dst):
        copy = pltpu.make_async_copy(src, dst, load_sem.at[k])
        copy.start()
        return copy

    loads = [
        load(0, grad_hbm, grad),
        load(1, gate_hbm, gate),
        load(2, inner_hbm, inner),
        load(3, lane_rows_hbm, lane_rows),
        load(4, picked_hbm, picked),
        load(5, filt_hbm.at[:, plane], filt),
        load(6, spec_hbm, spec),
        load(7, lanes_hbm, lanes),
        load(8, wide_hbm, wide),
    ]

    barrier = pltpu.get_barrier_semaphore()
    for peer in peers:
        pl.semaphore_signal(barrier, inc=1, device_id={"ctx": peer}, device_id_type=MESH)
        pl.semaphore_signal(barrier, inc=1, device_id={"ctx": peer, "ch": other}, device_id_type=MESH)
    for step in range(1, 4):
        for side in range(2):
            there = 2 * ((plane + step) % 4) + side
            pl.semaphore_signal(barrier, inc=1, device_id={"ch": there}, device_id_type=MESH)
    pl.semaphore_signal(barrier, inc=1, device_id={"ch": other}, device_id_type=MESH)

    def send_all(k, out, into):
        for peer in peers:
            pltpu.make_async_remote_copy(
                out.at[peer], into.at[me], send_sem.at[k], recv_sem.at[k],
                device_id={"ctx": peer}, device_id_type=MESH,
            ).start()
        into[me] = out[me]

    def bulk(k, ref):
        return pltpu.make_async_remote_copy(
            ref, ref, send_sem.at[k], recv_sem.at[k], device_id={"ctx": (me + 1) % SHARDS}, device_id_type=MESH
        )

    def arrived(k, into):
        bulk(k, into.at[pl.ds(0, SHARDS - 1)]).wait_recv()

    def left(k, out):
        bulk(k, out.at[pl.ds(0, SHARDS - 1)]).wait_send()

    loads[0].wait()
    loads[1].wait()
    x_out[...] = (grad[...] * gate[...]).reshape(SHARDS, 32, LANES)

    for k in (2, 3, 4):
        loads[k].wait()
    lane_ids = lax.broadcasted_iota(jnp.int32, (WIDE, LANES), 1)
    for b in range(2):
        row = 2 * me + b
        for ri in range(2):
            column = jnp.sum(jnp.where(lane_ids == row + RADIX * ri, picked[...], 0.0), axis=1, keepdims=True)
            pre[b, ri] = jnp.broadcast_to(column, (WIDE, LANES))
        vr = lane_rows[0, pl.ds(row, 1), :]
        vi = lane_rows[1, pl.ds(row, 1), :]
        tr = inner[0] * vr - inner[1] * vi
        ti = inner[0] * vi + inner[1] * vr
        mid[b, 0] = tr
        mid[b, 1] = ti
        midt[b, 0] = tr.T * 0.5
        midt[b, 1] = ti.T * 0.5

    def spread(ref, b):
        return jnp.concatenate([ref[pl.ds(2 * s + b, LANES, stride=4), :] for s in range(2)], axis=1)

    loads[5].wait()
    loads[6].wait()
    for b in range(2):
        prods[b, 0, 0], prods[b, 0, 1] = spread(filt.at[0], b), spread(filt.at[1], b)
        for ch in range(2):
            prods[b, 1 + ch, 0], prods[b, 1 + ch, 1] = spread(spec.at[0, ch], b), spread(spec.at[1, ch], b)
    loads[7].wait()
    loads[8].wait()

    def inverse_rows(b, arrays):
        mr, mi = midt[b, 0], midt[b, 1]
        stacked = []
        for re, im in arrays:
            c = product(lanes[1], jnp.concatenate([re, im], axis=0))
            cr, ci = c[:LANES], c[LANES:]
            stacked.append(jnp.concatenate([cr * mr + ci * mi, ci * mr - cr * mi], axis=1))
        t = product(wide[1], jnp.concatenate(stacked, axis=0) if len(stacked) > 1 else stacked[0], nt=True)
        pr, pi = pre[b, 0], pre[b, 1]
        out = []
        for k in range(len(arrays)):
            sr = t[:WIDE, LANES * k : LANES * (k + 1)]
            si = t[WIDE:, LANES * k : LANES * (k + 1)]
            out.append((sr * pr + si * pi, si * pr - sr * pi))
        return out

    pl.semaphore_wait(barrier, 2 * SHARDS - 1 + 6)

    send_all(0, x_out, x_in)

    def conv_row(b):
        hr, hi = prods[b, 0, 0], prods[b, 0, 1]
        arrays = []
        for ch in range(2):
            ur, ui = prods[b, 1 + ch, 0], prods[b, 1 + ch, 1]
            arrays.append((ur * hr - ui * hi, ur * hi + ui * hr))
        for ch, (re, im) in enumerate(inverse_rows(b, arrays)):
            c_out[b, :, 0, ch] = re.reshape(SHARDS, 16, LANES)
            c_out[b, :, 1, ch] = im.reshape(SHARDS, 16, LANES)

    def slab_forward(step, carry):
        ch, half = step // 2, step % 2
        xs = [x_in[j, pl.ds(16 * half + ch, 8, stride=2), :] for j in range(SHARDS)]
        ys = real_dft(xs + [None] * SHARDS)
        at = pl.ds(pl.multiple_of(8 * half, 8), 8)
        for r in range(RADIX):
            re, im = ys[min(r, RADIX - r)]
            if im is None:
                im = jnp.zeros_like(re)
            elif r > RADIX // 2:
                im = -im
            y_out[r % 2, r // 2, 0, ch, at, :] = re
            y_out[r % 2, r // 2, 1, ch, at, :] = im
        return carry

    def conv_step(step, carry):
        conv_row(step)

        @pl.when(step == 0)
        def _():
            send_all(3, c_out.at[0], c_in.at[0])
            arrived(0, x_in)
            lax.fori_loop(0, 4, slab_forward, 0)
            for turn in range(2):
                b = (1 - core + turn) % 2
                send_all(1 + turn, y_out.at[b], y_in.at[b])

        return carry

    lax.fori_loop(0, 2, conv_step, 0)
    send_all(4, c_out.at[1], c_in.at[1])

    swap = pltpu.make_async_remote_copy(
        fsum.at[1 - core], fpart, send_sem.at[5], recv_sem.at[5], device_id={"ch": other}, device_id_type=MESH
    )

    def forward_row(turn, carry):
        b = (1 - core + turn) % 2
        bulk(1 + turn, y_in.at[b, pl.ds(0, SHARDS - 1)]).wait_recv()
        pr = jnp.concatenate([pre[b, 0]] * 2, axis=1)
        pi = jnp.concatenate([pre[b, 1]] * 2, axis=1)
        yr = jnp.concatenate([y_in[b, :, 0, ch].reshape(WIDE, LANES) for ch in range(2)], axis=1)
        yi = jnp.concatenate([y_in[b, :, 1, ch].reshape(WIDE, LANES) for ch in range(2)], axis=1)
        a = product(wide[0], jnp.concatenate([yr * pr - yi * pi, yr * pi + yi * pr], axis=0))
        mr, mi = mid[b, 0], mid[b, 1]
        fr = fi = None
        for ch in range(2):
            ar = a[:WIDE, LANES * ch : LANES * (ch + 1)]
            ai = a[WIDE:, LANES * ch : LANES * (ch + 1)]
            g = product(lanes[0], jnp.concatenate([ar * mr - ai * mi, ar * mi + ai * mr], axis=1), nt=True)
            gr, gi = g[:LANES], g[LANES:]
            ur, ui = prods[b, 1 + ch, 0], prods[b, 1 + ch, 1]
            wr, wi = ur * gr + ui * gi, ur * gi - ui * gr
            fr, fi = (wr, wi) if ch == 0 else (fr + wr, fi + wi)
            hr, hi = prods[b, 0, 0], prods[b, 0, 1]
            prods[b, 1 + ch, 0], prods[b, 1 + ch, 1] = hr * gr + hi * gi, hr * gi - hi * gr
        fsum[b, 0], fsum[b, 1] = fr, fi

        @pl.when(turn == 0)
        def _():
            swap.start()

        return carry

    lax.fori_loop(0, 2, forward_row, 0)
    swap.wait_recv()
    ((re, im),) = inverse_rows(core, [(fsum[core, 0] + fpart[0], fsum[core, 1] + fpart[1])])
    f_out[:, 0] = re.reshape(2 * SHARDS, 8, LANES)
    f_out[:, 1] = im.reshape(2 * SHARDS, 8, LANES)
    for peer in peers + [me]:
        for side in range(2):
            if peer is me and side == 0:
                continue
            there = other if side else group
            half = 1 - core if side else core
            pltpu.make_async_remote_copy(
                f_out.at[2 * peer + half], f_in.at[2 * me + core], send_sem.at[6], recv_sem.at[6],
                device_id={"ctx": peer, "ch": there}, device_id_type=MESH,
            ).start()
    f_in[2 * me + core] = f_out[2 * me + core]

    def input_row(b, carry):
        arrays = [(prods[b, 1 + ch, 0], prods[b, 1 + ch, 1]) for ch in range(2)]
        for ch, both in enumerate(inverse_rows(b, arrays)):
            for ri in range(2):
                pieces = both[ri].reshape(SHARDS, 16, LANES)
                for half in range(2):
                    i_out[half, :, b, ri, ch] = pieces[:, 8 * half : 8 * half + 8]
        return carry

    lax.fori_loop(0, 2, input_row, 0)
    send_all(7, i_out.at[0], i_in.at[0])

    bulk(6, f_in.at[pl.ds(0, 2 * SHARDS - 1)]).wait_recv()
    ws = [(f_in[r, 0], f_in[r, 1]) for r in range(RADIX)]
    for j, (re, _) in enumerate(back_dft(ws, first_half=True)):
        g_out[j] = re + re
    send_all(10, g_out, g_in)
    send_all(8, i_out.at[1], i_in.at[1])

    def slab_back(row, put):
        ws = [None] * RADIX
        for r in range(RADIX // 2 + 1):
            q = (RADIX - r) % RADIX
            a = row(r, 0, 0) + row(q, 0, 0)
            c = row(r, 0, 1) + row(q, 0, 1)
            if q == r:
                ws[r] = (a, c)
                continue
            bb = row(r, 1, 0) - row(q, 1, 0)
            d = row(r, 1, 1) - row(q, 1, 1)
            ws[r] = (a - d, bb + c)
            ws[q] = (a + d, c - bb)
        for j, (re, im) in enumerate(back_dft(ws, first_half=True)):
            put(j, 0, re)
            put(j, 1, im)

    def conv_back(half, carry):
        at = pl.ds(pl.multiple_of(8 * half, 8), 8)

        def put(j, ch, value):
            d_out[j, pl.ds(16 * half + ch, 8, stride=2), :] = value

        slab_back(lambda r, ri, ch: c_in[r % 2, r // 2, ri, ch, at, :], put)
        return carry

    arrived(3, c_in.at[0])
    arrived(4, c_in.at[1])
    lax.fori_loop(0, 2, conv_back, 0)
    send_all(9, d_out, d_in)

    def input_back(half, carry):
        bulk(7 + half, i_in.at[half, pl.ds(0, SHARDS - 1)]).wait_recv()

        def put(j, ch, value):
            e_out[half, j, pl.ds(ch, 8, stride=2), :] = value

        slab_back(lambda r, ri, ch: i_in[half, r // 2, r % 2, ri, ch], put)
        for peer in peers:
            pltpu.make_async_remote_copy(
                e_out.at[half, peer], e_in.at[me, half], send_sem.at[11 + half], recv_sem.at[11 + half],
                device_id={"ctx": peer}, device_id_type=MESH,
            ).start()
        e_in[me, half] = e_out[half, me]

        @pl.when(half == 0)
        def _():
            arrived(10, g_in)
            for step in range(4):
                for side in range(2):
                    if step == 0 and side == 0:
                        continue
                    there = 2 * ((plane + step) % 4) + (1 - core if side else core)
                    pltpu.make_async_remote_copy(
                        g_in, g_all.at[group], send_sem.at[13], recv_sem.at[13],
                        device_id={"ch": there}, device_id_type=MESH,
                    ).start()
            g_all[group] = g_in[...]

        return carry

    lax.fori_loop(0, 2, input_back, 0)

    arrived(9, d_in)
    gate[...] = grad[...] * d_in[...].reshape(512, LANES)
    store_gg = load(1, gate, gg_out)
    bulk(13, g_all.at[pl.ds(0, 7)]).wait_recv()
    for f in range(FILTERS):
        for c in range(2):
            for q in range(SHARDS):
                gf[pl.ds(64 * q + 32 * c + f, 8, stride=4), :] = g_all[2 * f + c, q]
    store_gf = load(2, gf, gf_out)
    bulk(11, e_out.at[0, pl.ds(0, SHARDS - 1)]).wait_recv()
    bulk(12, e_out.at[1, pl.ds(0, SHARDS - 1)]).wait_recv()
    store_gi = load(0, e_in, gi_out)

    left(0, x_out)
    for turn in range(2):
        left(1 + turn, y_out.at[turn])
        left(3 + turn, c_out.at[turn])
        left(7 + turn, i_out.at[turn])
        left(11 + turn, e_out.at[turn])
    swap.wait_send()
    bulk(6, f_out.at[pl.ds(0, 2 * SHARDS - 1)]).wait_send()
    left(9, d_out)
    left(10, g_out)
    bulk(13, g_all.at[pl.ds(0, 7)]).wait_send()
    store_gg.wait()
    store_gf.wait()
    store_gi.wait()


def store_results(*refs):
    ins, outs, sem = refs[:3], refs[3:6], refs[6]
    copies = [pltpu.make_async_copy(src, dst, sem.at[k]) for k, (src, dst) in enumerate(zip(ins, outs))]
    for copy in copies:
        copy.start()
    for copy in copies:
        copy.wait()


def per_device(grad_out, gate_in, input_spectrum, filter_spectrum):
    def tiled(x):
        lead = x.shape[:-2]
        pieces = x.reshape(*lead, x.shape[-2], WIDE, LANES)
        return jnp.swapaxes(pieces, -3, -2).reshape(*lead, WIDE * x.shape[-2], LANES)

    def untiled(x, rows):
        return jnp.swapaxes(x.reshape(WIDE, rows, LANES), 0, 1).reshape(rows, COLS)

    consts = tables()
    operands = (tiled(grad_out), tiled(gate_in), tiled(input_spectrum), tiled(filter_spectrum), *consts)
    slab = lambda *dims: pltpu.VMEM((SHARDS, *dims, LANES), F32)
    wave = pltpu.VMEM((2, SHARDS, 2, 2, 16, LANES), F32)
    half_wave = pltpu.VMEM((2, SHARDS, 2, 2, 2, 8, LANES), F32)
    scratch = [
        pltpu.VMEM((512, LANES), F32),
        pltpu.VMEM((512, LANES), F32),
        pltpu.VMEM((2, 2, 512, LANES), F32),
        pltpu.VMEM((2, 512, LANES), F32),
        *[pltpu.VMEM(c.shape, c.dtype) for c in consts],
        pltpu.VMEM((2, 2, WIDE, LANES), F32),
        pltpu.VMEM((2, 2, WIDE, LANES), F32),
        pltpu.VMEM((2, 2, LANES, WIDE), F32),
        slab(32),
        slab(32),
        wave,
        wave,
        wave,
        wave,
        half_wave,
        half_wave,
        slab(32),
        slab(32),
        pltpu.VMEM((2, SHARDS, 16, LANES), F32),
        pltpu.VMEM((SHARDS, 2, 16, LANES), F32),
        pltpu.VMEM((2, 3, 2, LANES, WIDE), F32),
        pltpu.VMEM((2, 2, LANES, WIDE), F32),
        pltpu.VMEM((2, LANES, WIDE), F32),
        pltpu.VMEM((2 * SHARDS, 2, 8, LANES), F32),
        pltpu.VMEM((2 * SHARDS, 2, 8, LANES), F32),
        slab(8),
        slab(8),
        pltpu.VMEM((8, SHARDS, 8, LANES), F32),
        pltpu.VMEM((1024, LANES), F32),
        pltpu.SemaphoreType.DMA((9,)),
        pltpu.SemaphoreType.DMA((14,)),
        pltpu.SemaphoreType.DMA((14,)),
    ]
    in_hbm = pl.BlockSpec(memory_space=pltpu.HBM)
    anywhere = pl.BlockSpec(memory_space=pl.ANY)
    results = [
        jax.ShapeDtypeStruct((SHARDS, 2, 16, LANES), F32),
        jax.ShapeDtypeStruct((512, LANES), F32),
        jax.ShapeDtypeStruct((1024, LANES), F32),
    ]
    found = pl.pallas_call(
        kernel,
        out_shape=results,
        in_specs=[in_hbm] * len(operands),
        out_specs=[anywhere] * 3,
        scratch_shapes=scratch,
        compiler_params=pltpu.CompilerParams(
            collective_id=0, has_side_effects=True, vmem_limit_bytes=40 * 2**20
        ),
        name="gated_conv_back",
    )(*[pltpu.with_memory_space_constraint(x, pltpu.HBM) for x in operands])
    grad_input, grad_gate, grad_filter = pl.pallas_call(
        store_results,
        out_shape=results,
        in_specs=[anywhere] * 3,
        out_specs=[in_hbm] * 3,
        scratch_shapes=[pltpu.SemaphoreType.DMA((3,))],
        compiler_params=pltpu.CompilerParams(vmem_limit_bytes=2**20),
        name="store_results",
    )(*found)
    return (
        untiled(grad_input.reshape(512, LANES), 2),
        untiled(grad_gate, 2),
        untiled(grad_filter, 4),
    )


def solution(mesh):
    return jax.shard_map(
        per_device,
        mesh=mesh,
        in_specs=(
            P("ch", "ctx"),
            P("ch", "ctx"),
            P(None, "ch", "ctx", None),
            P(None, None, "ctx", None),
        ),
        out_specs=(P("ch", "ctx"), P("ch", "ctx"), P(None, "ctx")),
        check_vma=False,
    )
```

```python
from functools import partial
import math

import jax
import jax.numpy as jnp
import numpy as np
from jax import lax
from jax.experimental import pallas as pl
from jax.experimental.pallas import tpu as pltpu
from jax.sharding import PartitionSpec as P

CHANNELS = 16
FILTERS = 4
RADIX = 32
COLS = 32768
TOTAL = RADIX * COLS
SHARDS = 16
WIDE = 256
LANES = 128
MESH = pl.DeviceIdType.MESH
STEPS = (
    (2, 2), (2, 1), (1, 2), (2, 3), (3, 2), (2, 0), (0, 2),
    (1, 1), (3, 3), (1, 3), (3, 1), (1, 0), (0, 1), (3, 0), (0, 3),
)
F32 = jnp.float32
BF16 = jnp.bfloat16


def real_form(matrix):
    return np.block([[matrix.real, -matrix.imag], [matrix.imag, matrix.real]])


def halves(matrix):
    whole = matrix.astype(np.float32)
    high = whole.astype(jnp.bfloat16)
    low = (matrix - high.astype(np.float64)).astype(np.float32).astype(jnp.bfloat16)
    return np.stack([high, low])


def tables():
    def unit(counts, modulus):
        return np.exp(-2j * np.pi * (counts % modulus) / modulus)

    wide = np.arange(WIDE)
    lanes = np.arange(LANES)
    rows = np.arange(RADIX)
    dft_wide = unit(wide[:, None] * wide[None, :], WIDE)
    dft_lanes = unit(lanes[:, None] * lanes[None, :], LANES)
    inner = unit(wide[:, None] * lanes[None, :], COLS) * 2.0**-10
    lane_rows = unit(rows[:, None] * lanes[None, :], TOTAL)
    wide_rows = unit(wide[:, None] * rows[None, :], TOTAL // LANES)
    picked = np.concatenate([wide_rows.real, wide_rows.imag, np.zeros((WIDE, LANES - 2 * RADIX))], axis=1)
    return (
        np.stack([halves(real_form(dft_wide)), halves(real_form(dft_wide.conj()))]),
        np.stack([halves(real_form(dft_lanes)), halves(real_form(dft_lanes.conj()))]),
        np.stack([inner.real, inner.imag]).astype(np.float32),
        np.stack([lane_rows.real, lane_rows.imag]).astype(np.float32),
        picked.astype(np.float32),
    )


def times_unit(value, turn):
    re, im = value
    turn = turn % 1.0
    if turn == 0.0:
        return re, im
    if turn == 0.5:
        return negated(re), negated(im)
    if turn == 0.25:
        return negated(im), re
    if turn == 0.75:
        return im, negated(re)
    c, s = math.cos(2 * math.pi * turn), math.sin(2 * math.pi * turn)
    if im is None:
        return re * c, re * s
    if re is None:
        return im * (-s), im * c
    if turn in (0.125, 0.375, 0.625, 0.875):
        h = math.sqrt(0.5)
        if turn == 0.125:
            return (re - im) * h, (re + im) * h
        if turn == 0.375:
            return (re + im) * (-h), (re - im) * h
        if turn == 0.625:
            return (im - re) * h, (re + im) * (-h)
        return (re + im) * h, (im - re) * h
    return re * c - im * s, re * s + im * c


def negated(x):
    return None if x is None else -x


def plus(a, b):
    if a is None:
        return b
    return a if b is None else a + b


def minus(a, b):
    if b is None:
        return a
    return -b if a is None else a - b


def real_dft(xs):
    n = len(xs)
    if n == 1:
        return [(xs[0], None)]
    even, odd = real_dft(xs[0::2]), real_dft(xs[1::2])
    if n == 2:
        a, b = even[0][0], odd[0][0]
        return [(plus(a, b), None), (minus(a, b), None)]
    out = [None] * (n // 2 + 1)
    for k in range(n // 4 + 1):
        e, t = even[k], times_unit(odd[k], -k / n)
        out[k] = (plus(e[0], t[0]), plus(e[1], t[1]))
        if n // 2 - k != k:
            out[n // 2 - k] = (minus(e[0], t[0]), minus(t[1], e[1]))
    return out


def back_dft(xs, first_half=False):
    n = len(xs)
    if n == 1:
        return list(xs)
    even, odd = back_dft(xs[0::2]), back_dft(xs[1::2])
    upper, lower = [], []
    for k in range(n // 2):
        e, t = even[k], times_unit(odd[k], k / n)
        upper.append((e[0] + t[0], e[1] + t[1]))
        if not first_half:
            lower.append((e[0] - t[0], e[1] - t[1]))
    return upper + lower


def parts(x):
    high = x.astype(BF16)
    return high, (x - high.astype(F32)).astype(BF16)


def product(left, x, nt=False):
    high, low = parts(x)
    dims = (((1,), (1 if nt else 0,)), ((), ()))
    dot = partial(lax.dot_general, dimension_numbers=dims, preferred_element_type=F32)
    return dot(left[0], high) + (dot(left[0], low) + dot(left[1], high))


def kernel(
    grad_hbm, gate_hbm, spec_hbm, filt_hbm, wide_hbm, lanes_hbm, inner_hbm, lane_rows_hbm, picked_hbm,
    gi_out, gg_out, gf_out,
    grad, gate, spec, filt, wide, lanes, inner, lane_rows, picked,
    pre, mid, midt,
    x_out, x_in, y_out, y_in, c_out, c_in, i_out, i_in, d_out, d_in, e_out,
    prods, fsum, fpart, f_out, f_in, g_out, g_in, g_all, gf,
    load_sem, send_sem, recv_sem,
):
    me = lax.axis_index("ctx")
    group = lax.axis_index("ch")
    core = group % 2
    plane = group // 2
    other = group + 1 - 2 * core
    peers = [(me // 4 + dx) % 4 * 4 + (me + dz) % 4 for dx, dz in STEPS]

    barrier = pltpu.get_barrier_semaphore()
    for peer in peers:
        pl.semaphore_signal(barrier, inc=1, device_id={"ctx": peer}, device_id_type=MESH)
        pl.semaphore_signal(barrier, inc=1, device_id={"ctx": peer, "ch": other}, device_id_type=MESH)
    for step in range(1, 4):
        for side in range(2):
            there = 2 * ((plane + step) % 4) + side
            pl.semaphore_signal(barrier, inc=1, device_id={"ch": there}, device_id_type=MESH)
    pl.semaphore_signal(barrier, inc=1, device_id={"ch": other}, device_id_type=MESH)

    def load(k, src, dst):
        copy = pltpu.make_async_copy(src, dst, load_sem.at[k])
        copy.start()
        return copy

    loads = [
        load(0, grad_hbm, grad),
        load(1, gate_hbm, gate),
        load(2, inner_hbm, inner),
        load(3, lane_rows_hbm, lane_rows),
        load(4, picked_hbm, picked),
        load(5, filt_hbm.at[:, plane], filt),
        load(6, spec_hbm, spec),
        load(7, lanes_hbm, lanes),
        load(8, wide_hbm, wide),
    ]

    def send_all(k, out, into):
        for peer in peers:
            pltpu.make_async_remote_copy(
                out.at[peer], into.at[me], send_sem.at[k], recv_sem.at[k],
                device_id={"ctx": peer}, device_id_type=MESH,
            ).start()
        into[me] = out[me]

    def bulk(k, ref):
        return pltpu.make_async_remote_copy(
            ref, ref, send_sem.at[k], recv_sem.at[k], device_id={"ctx": (me + 1) % SHARDS}, device_id_type=MESH
        )

    def arrived(k, into):
        bulk(k, into.at[pl.ds(0, SHARDS - 1)]).wait_recv()

    def left(k, out):
        bulk(k, out.at[pl.ds(0, SHARDS - 1)]).wait_send()

    loads[0].wait()
    loads[1].wait()
    x_out[...] = (grad[...] * gate[...]).reshape(SHARDS, 32, LANES)

    for k in (2, 3, 4):
        loads[k].wait()
    lane_ids = lax.broadcasted_iota(jnp.int32, (WIDE, LANES), 1)
    for b in range(2):
        row = 2 * me + b
        for ri in range(2):
            column = jnp.sum(jnp.where(lane_ids == row + RADIX * ri, picked[...], 0.0), axis=1, keepdims=True)
            pre[b, ri] = jnp.broadcast_to(column, (WIDE, LANES))
        vr = lane_rows[0, pl.ds(row, 1), :]
        vi = lane_rows[1, pl.ds(row, 1), :]
        tr = inner[0] * vr - inner[1] * vi
        ti = inner[0] * vi + inner[1] * vr
        mid[b, 0] = tr
        mid[b, 1] = ti
        midt[b, 0] = tr.T * 0.5
        midt[b, 1] = ti.T * 0.5

    def spread(ref, b):
        return jnp.concatenate([ref[pl.ds(2 * s + b, LANES, stride=4), :] for s in range(2)], axis=1)

    loads[5].wait()
    loads[6].wait()
    for b in range(2):
        prods[b, 0, 0], prods[b, 0, 1] = spread(filt.at[0], b), spread(filt.at[1], b)
        for ch in range(2):
            prods[b, 1 + ch, 0], prods[b, 1 + ch, 1] = spread(spec.at[0, ch], b), spread(spec.at[1, ch], b)
    loads[7].wait()
    loads[8].wait()

    def inverse_rows(b, arrays):
        mr, mi = midt[b, 0], midt[b, 1]
        stacked = []
        for re, im in arrays:
            c = product(lanes[1], jnp.concatenate([re, im], axis=0))
            cr, ci = c[:LANES], c[LANES:]
            stacked.append(jnp.concatenate([cr * mr + ci * mi, ci * mr - cr * mi], axis=1))
        t = product(wide[1], jnp.concatenate(stacked, axis=0) if len(stacked) > 1 else stacked[0], nt=True)
        pr, pi = pre[b, 0], pre[b, 1]
        out = []
        for k in range(len(arrays)):
            sr = t[:WIDE, LANES * k : LANES * (k + 1)]
            si = t[WIDE:, LANES * k : LANES * (k + 1)]
            out.append((sr * pr + si * pi, si * pr - sr * pi))
        return out

    pl.semaphore_wait(barrier, 2 * SHARDS - 1 + 6)

    send_all(0, x_out, x_in)

    def conv_row(b):
        hr, hi = prods[b, 0, 0], prods[b, 0, 1]
        arrays = []
        for ch in range(2):
            ur, ui = prods[b, 1 + ch, 0], prods[b, 1 + ch, 1]
            arrays.append((ur * hr - ui * hi, ur * hi + ui * hr))
        for ch, (re, im) in enumerate(inverse_rows(b, arrays)):
            c_out[b, :, 0, ch] = re.reshape(SHARDS, 16, LANES)
            c_out[b, :, 1, ch] = im.reshape(SHARDS, 16, LANES)

    def slab_forward(step, carry):
        ch, half = step // 2, step % 2
        xs = [x_in[j, pl.ds(16 * half + ch, 8, stride=2), :] for j in range(SHARDS)]
        ys = real_dft(xs + [None] * SHARDS)
        at = pl.ds(pl.multiple_of(8 * half, 8), 8)
        for r in range(RADIX):
            re, im = ys[min(r, RADIX - r)]
            if im is None:
                im = jnp.zeros_like(re)
            elif r > RADIX // 2:
                im = -im
            y_out[r % 2, r // 2, 0, ch, at, :] = re
            y_out[r % 2, r // 2, 1, ch, at, :] = im
        return carry

    def conv_step(step, carry):
        conv_row(step)

        @pl.when(step == 0)
        def _():
            send_all(3, c_out.at[0], c_in.at[0])
            arrived(0, x_in)
            lax.fori_loop(0, 4, slab_forward, 0)
            for turn in range(2):
                b = (1 - core + turn) % 2
                send_all(1 + turn, y_out.at[b], y_in.at[b])

        return carry

    lax.fori_loop(0, 2, conv_step, 0)
    send_all(4, c_out.at[1], c_in.at[1])

    swap = pltpu.make_async_remote_copy(
        fsum.at[1 - core], fpart, send_sem.at[5], recv_sem.at[5], device_id={"ch": other}, device_id_type=MESH
    )

    def forward_row(turn):
        b = (1 - core + turn) % 2
        bulk(1 + turn, y_in.at[b, pl.ds(0, SHARDS - 1)]).wait_recv()
        pr = jnp.concatenate([pre[b, 0]] * 2, axis=1)
        pi = jnp.concatenate([pre[b, 1]] * 2, axis=1)
        yr = jnp.concatenate([y_in[b, :, 0, ch].reshape(WIDE, LANES) for ch in range(2)], axis=1)
        yi = jnp.concatenate([y_in[b, :, 1, ch].reshape(WIDE, LANES) for ch in range(2)], axis=1)
        a = product(wide[0], jnp.concatenate([yr * pr - yi * pi, yr * pi + yi * pr], axis=0))
        mr, mi = mid[b, 0], mid[b, 1]
        fr = fi = None
        for ch in range(2):
            ar = a[:WIDE, LANES * ch : LANES * (ch + 1)]
            ai = a[WIDE:, LANES * ch : LANES * (ch + 1)]
            g = product(lanes[0], jnp.concatenate([ar * mr - ai * mi, ar * mi + ai * mr], axis=1), nt=True)
            gr, gi = g[:LANES], g[LANES:]
            ur, ui = prods[b, 1 + ch, 0], prods[b, 1 + ch, 1]
            wr, wi = ur * gr + ui * gi, ur * gi - ui * gr
            fr, fi = (wr, wi) if ch == 0 else (fr + wr, fi + wi)
            hr, hi = prods[b, 0, 0], prods[b, 0, 1]
            prods[b, 1 + ch, 0], prods[b, 1 + ch, 1] = hr * gr + hi * gi, hr * gi - hi * gr
        fsum[b, 0], fsum[b, 1] = fr, fi

        return b

    def input_row(b):
        arrays = [(prods[b, 1 + ch, 0], prods[b, 1 + ch, 1]) for ch in range(2)]
        for ch, both in enumerate(inverse_rows(b, arrays)):
            for ri in range(2):
                pieces = both[ri].reshape(SHARDS, 16, LANES)
                for half in range(2):
                    i_out[b, :, half, ri, ch] = pieces[:, 8 * half : 8 * half + 8]

    def filter_row():
        swap.wait_recv()
        ((re, im),) = inverse_rows(core, [(fsum[core, 0] + fpart[0], fsum[core, 1] + fpart[1])])
        f_out[:, 0] = re.reshape(2 * SHARDS, 8, LANES)
        f_out[:, 1] = im.reshape(2 * SHARDS, 8, LANES)
        for peer in peers + [me]:
            for side in range(2):
                if peer is me and side == 0:
                    continue
                there = other if side else group
                half = 1 - core if side else core
                pltpu.make_async_remote_copy(
                    f_out.at[2 * peer + half], f_in.at[2 * me + core], send_sem.at[6], recv_sem.at[6],
                    device_id={"ctx": peer, "ch": there}, device_id_type=MESH,
                ).start()
        f_in[2 * me + core] = f_out[2 * me + core]

    def row_turn(turn, carry):
        b = forward_row(turn)

        @pl.when(turn == 0)
        def _():
            swap.start()

        @pl.when(turn == 1)
        def _():
            filter_row()

        input_row(b)

        @pl.when(turn == 0)
        def _():
            send_all(7, i_out.at[1 - core], i_in.at[1 - core])

        return carry

    lax.fori_loop(0, 2, row_turn, 0)
    for peer in peers:
        pltpu.make_async_remote_copy(
            i_out.at[core, peer, 0], i_in.at[core, me, 0], send_sem.at[8], recv_sem.at[8],
            device_id={"ctx": peer}, device_id_type=MESH,
        ).start()
    i_in[core, me] = i_out[core, me]

    def slab_back(row, put):
        ws = [None] * RADIX
        for r in range(RADIX // 2 + 1):
            q = (RADIX - r) % RADIX
            a = row(r, 0, 0) + row(q, 0, 0)
            c = row(r, 0, 1) + row(q, 0, 1)
            if q == r:
                ws[r] = (a, c)
                continue
            bb = row(r, 1, 0) - row(q, 1, 0)
            d = row(r, 1, 1) - row(q, 1, 1)
            ws[r] = (a - d, bb + c)
            ws[q] = (a + d, c - bb)
        for j, (re, im) in enumerate(back_dft(ws, first_half=True)):
            put(j, 0, re)
            put(j, 1, im)

    def conv_back(half, carry):
        at = pl.ds(pl.multiple_of(8 * half, 8), 8)

        def put(j, ch, value):
            d_out[j, pl.ds(16 * half + ch, 8, stride=2), :] = value

        slab_back(lambda r, ri, ch: c_in[r % 2, r // 2, ri, ch, at, :], put)
        return carry

    arrived(3, c_in.at[0])
    arrived(4, c_in.at[1])
    lax.fori_loop(0, 2, conv_back, 0)
    send_all(9, d_out, d_in)

    bulk(6, f_in.at[pl.ds(0, 2 * SHARDS - 1)]).wait_recv()
    ws = [(f_in[r, 0], f_in[r, 1]) for r in range(RADIX)]
    for j, (re, _) in enumerate(back_dft(ws, first_half=True)):
        g_out[j] = re + re
    send_all(10, g_out, g_in)
    for peer in peers:
        pltpu.make_async_remote_copy(
            i_out.at[core, peer, 1], i_in.at[core, me, 1], send_sem.at[15], recv_sem.at[15],
            device_id={"ctx": peer}, device_id_type=MESH,
        ).start()

    arrived(7, i_in.at[1 - core])

    def half_of(ref, half):
        return ref.at[core, pl.ds(0, SHARDS - 1), half]

    share = pltpu.make_async_remote_copy(
        g_all.at[core], g_all.at[core], send_sem.at[14], recv_sem.at[14],
        device_id={"ch": other}, device_id_type=MESH,
    )

    def input_back(half, carry):
        bulk(8 + 7 * half, half_of(i_in, half)).wait_recv()

        def put(j, ch, value):
            e_out[half, j, pl.ds(ch, 8, stride=2), :] = value

        slab_back(lambda r, ri, ch: i_in[r % 2, r // 2, half, ri, ch], put)
        for peer in peers:
            pltpu.make_async_remote_copy(
                e_out.at[half, peer], gi_out.at[me, half], send_sem.at[11 + half], recv_sem.at[11 + half],
                device_id={"ctx": peer}, device_id_type=MESH,
            ).start()
        own = pltpu.make_async_copy(e_out.at[half, me], gi_out.at[me, half], load_sem.at[half])
        own.start()

        @pl.when(half == 0)
        def _():
            arrived(10, g_in)
            for step in range(1, 4):
                pltpu.make_async_remote_copy(
                    g_in, g_all.at[core, plane], send_sem.at[13], recv_sem.at[13],
                    device_id={"ch": 2 * ((plane + step) % 4) + core}, device_id_type=MESH,
                ).start()
            g_all[core, plane] = g_in[...]

        @pl.when(half == 1)
        def _():
            bulk(13, g_all.at[core, pl.ds(0, 3)]).wait_recv()
            share.start()

        own.wait()
        return carry

    lax.fori_loop(0, 2, input_back, 0)

    arrived(9, d_in)
    gate[...] = grad[...] * d_in[...].reshape(512, LANES)
    store_gg = load(2, gate, gg_out)
    share.wait_recv()
    for f in range(FILTERS):
        for c in range(2):
            for q in range(SHARDS):
                gf[pl.ds(64 * q + 32 * c + f, 8, stride=4), :] = g_all[c, f, q]
    store_gf = load(3, gf, gf_out)
    bulk(11, e_out.at[0, pl.ds(0, SHARDS - 1)]).wait_recv()
    bulk(12, e_out.at[1, pl.ds(0, SHARDS - 1)]).wait_recv()

    left(0, x_out)
    for turn in range(2):
        left(1 + turn, y_out.at[turn])
        left(3 + turn, c_out.at[turn])
        bulk(8 + 7 * turn, half_of(i_out, turn)).wait_send()
        left(11 + turn, e_out.at[turn])
    swap.wait_send()
    bulk(6, f_out.at[pl.ds(0, 2 * SHARDS - 1)]).wait_send()
    left(7, i_out.at[1 - core])
    left(9, d_out)
    left(10, g_out)
    bulk(13, g_all.at[core, pl.ds(0, 3)]).wait_send()
    share.wait_send()
    store_gg.wait()
    store_gf.wait()


def store_results(*refs):
    ins, outs, sem = refs[:3], refs[3:6], refs[6]
    copies = [pltpu.make_async_copy(src, dst, sem.at[k]) for k, (src, dst) in enumerate(zip(ins, outs))]
    for copy in copies:
        copy.start()
    for copy in copies:
        copy.wait()


def per_device(grad_out, gate_in, input_spectrum, filter_spectrum):
    def tiled(x):
        lead = x.shape[:-2]
        pieces = x.reshape(*lead, x.shape[-2], WIDE, LANES)
        return jnp.swapaxes(pieces, -3, -2).reshape(*lead, WIDE * x.shape[-2], LANES)

    def untiled(x, rows):
        return jnp.swapaxes(x.reshape(WIDE, rows, LANES), 0, 1).reshape(rows, COLS)

    consts = tables()
    operands = (tiled(grad_out), tiled(gate_in), tiled(input_spectrum), tiled(filter_spectrum), *consts)
    slab = lambda *dims: pltpu.VMEM((SHARDS, *dims, LANES), F32)
    wave = pltpu.VMEM((2, SHARDS, 2, 2, 16, LANES), F32)
    half_wave = pltpu.VMEM((2, SHARDS, 2, 2, 2, 8, LANES), F32)
    scratch = [
        pltpu.VMEM((512, LANES), F32),
        pltpu.VMEM((512, LANES), F32),
        pltpu.VMEM((2, 2, 512, LANES), F32),
        pltpu.VMEM((2, 512, LANES), F32),
        *[pltpu.VMEM(c.shape, c.dtype) for c in consts],
        pltpu.VMEM((2, 2, WIDE, LANES), F32),
        pltpu.VMEM((2, 2, WIDE, LANES), F32),
        pltpu.VMEM((2, 2, LANES, WIDE), F32),
        slab(32),
        slab(32),
        wave,
        wave,
        wave,
        wave,
        half_wave,
        half_wave,
        slab(32),
        slab(32),
        pltpu.VMEM((2, SHARDS, 16, LANES), F32),
        pltpu.VMEM((2, 3, 2, LANES, WIDE), F32),
        pltpu.VMEM((2, 2, LANES, WIDE), F32),
        pltpu.VMEM((2, LANES, WIDE), F32),
        pltpu.VMEM((2 * SHARDS, 2, 8, LANES), F32),
        pltpu.VMEM((2 * SHARDS, 2, 8, LANES), F32),
        slab(8),
        slab(8),
        pltpu.VMEM((2, 4, SHARDS, 8, LANES), F32),
        pltpu.VMEM((1024, LANES), F32),
        pltpu.SemaphoreType.DMA((9,)),
        pltpu.SemaphoreType.DMA((16,)),
        pltpu.SemaphoreType.DMA((16,)),
    ]
    in_hbm = pl.BlockSpec(memory_space=pltpu.HBM)
    anywhere = pl.BlockSpec(memory_space=pl.ANY)
    results = [
        jax.ShapeDtypeStruct((SHARDS, 2, 16, LANES), F32),
        jax.ShapeDtypeStruct((512, LANES), F32),
        jax.ShapeDtypeStruct((1024, LANES), F32),
    ]
    found = pl.pallas_call(
        kernel,
        out_shape=results,
        in_specs=[in_hbm] * len(operands),
        out_specs=[anywhere] * 3,
        scratch_shapes=scratch,
        compiler_params=pltpu.CompilerParams(
            collective_id=0, has_side_effects=True, vmem_limit_bytes=40 * 2**20
        ),
        name="gated_conv_back",
    )(*[pltpu.with_memory_space_constraint(x, pltpu.HBM) for x in operands])
    grad_input, grad_gate, grad_filter = pl.pallas_call(
        store_results,
        out_shape=results,
        in_specs=[anywhere] * 3,
        out_specs=[in_hbm] * 3,
        scratch_shapes=[pltpu.SemaphoreType.DMA((3,))],
        compiler_params=pltpu.CompilerParams(vmem_limit_bytes=2**20),
        name="store_results",
    )(*found)
    return (
        untiled(grad_input.reshape(512, LANES), 2),
        untiled(grad_gate, 2),
        untiled(grad_filter, 4),
    )


def solution(mesh):
    return jax.shard_map(
        per_device,
        mesh=mesh,
        in_specs=(
            P("ch", "ctx"),
            P("ch", "ctx"),
            P(None, "ch", "ctx", None),
            P(None, None, "ctx", None),
        ),
        out_specs=(P("ch", "ctx"), P("ch", "ctx"), P(None, "ctx")),
        check_vma=False,
    )
```

```python
from functools import partial
import math

import jax
import jax.numpy as jnp
import numpy as np
from jax import lax
from jax.experimental import pallas as pl
from jax.experimental.pallas import tpu as pltpu
from jax.sharding import PartitionSpec as P

CHANNELS = 16
FILTERS = 4
RADIX = 32
COLS = 32768
TOTAL = RADIX * COLS
SHARDS = 16
WIDE = 256
LANES = 128
MESH = pl.DeviceIdType.MESH
STEPS = (
    (2, 2), (2, 1), (1, 2), (2, 3), (3, 2), (2, 0), (0, 2),
    (1, 1), (3, 3), (1, 3), (3, 1), (1, 0), (0, 1), (3, 0), (0, 3),
)
F32 = jnp.float32
BF16 = jnp.bfloat16


def real_form(matrix):
    return np.block([[matrix.real, -matrix.imag], [matrix.imag, matrix.real]])


def halves(matrix):
    whole = matrix.astype(np.float32)
    high = whole.astype(jnp.bfloat16)
    low = (matrix - high.astype(np.float64)).astype(np.float32).astype(jnp.bfloat16)
    return np.stack([high, low])


def tables():
    def unit(counts, modulus):
        return np.exp(-2j * np.pi * (counts % modulus) / modulus)

    wide = np.arange(WIDE)
    lanes = np.arange(LANES)
    rows = np.arange(RADIX)
    dft_wide = unit(wide[:, None] * wide[None, :], WIDE)
    dft_lanes = unit(lanes[:, None] * lanes[None, :], LANES)
    inner = unit(wide[:, None] * lanes[None, :], COLS) * 2.0**-10
    lane_rows = unit(rows[:, None] * lanes[None, :], TOTAL)
    wide_rows = unit(wide[:, None] * rows[None, :], TOTAL // LANES)
    picked = np.concatenate([wide_rows.real, wide_rows.imag, np.zeros((WIDE, LANES - 2 * RADIX))], axis=1)
    return (
        np.stack([halves(real_form(dft_wide)), halves(real_form(dft_wide.conj()))]),
        np.stack([halves(real_form(dft_lanes)), halves(real_form(dft_lanes.conj()))]),
        np.stack([inner.real, inner.imag]).astype(np.float32),
        np.stack([lane_rows.real, lane_rows.imag]).astype(np.float32),
        picked.astype(np.float32),
    )


def times_unit(value, turn):
    re, im = value
    turn = turn % 1.0
    if turn == 0.0:
        return re, im
    if turn == 0.5:
        return negated(re), negated(im)
    if turn == 0.25:
        return negated(im), re
    if turn == 0.75:
        return im, negated(re)
    c, s = math.cos(2 * math.pi * turn), math.sin(2 * math.pi * turn)
    if im is None:
        return re * c, re * s
    if re is None:
        return im * (-s), im * c
    if turn in (0.125, 0.375, 0.625, 0.875):
        h = math.sqrt(0.5)
        if turn == 0.125:
            return (re - im) * h, (re + im) * h
        if turn == 0.375:
            return (re + im) * (-h), (re - im) * h
        if turn == 0.625:
            return (im - re) * h, (re + im) * (-h)
        return (re + im) * h, (im - re) * h
    return re * c - im * s, re * s + im * c


def negated(x):
    return None if x is None else -x


def plus(a, b):
    if a is None:
        return b
    return a if b is None else a + b


def minus(a, b):
    if b is None:
        return a
    return -b if a is None else a - b


def real_dft(xs):
    n = len(xs)
    if n == 1:
        return [(xs[0], None)]
    even, odd = real_dft(xs[0::2]), real_dft(xs[1::2])
    if n == 2:
        a, b = even[0][0], odd[0][0]
        return [(plus(a, b), None), (minus(a, b), None)]
    out = [None] * (n // 2 + 1)
    for k in range(n // 4 + 1):
        e, t = even[k], times_unit(odd[k], -k / n)
        out[k] = (plus(e[0], t[0]), plus(e[1], t[1]))
        if n // 2 - k != k:
            out[n // 2 - k] = (minus(e[0], t[0]), minus(t[1], e[1]))
    return out


def back_dft(xs, first_half=False):
    n = len(xs)
    if n == 1:
        return list(xs)
    even, odd = back_dft(xs[0::2]), back_dft(xs[1::2])
    upper, lower = [], []
    for k in range(n // 2):
        e, t = even[k], times_unit(odd[k], k / n)
        upper.append((e[0] + t[0], e[1] + t[1]))
        if not first_half:
            lower.append((e[0] - t[0], e[1] - t[1]))
    return upper + lower


def parts(x):
    high = x.astype(BF16)
    return high, (x - high.astype(F32)).astype(BF16)


def product(left, x, nt=False):
    high, low = parts(x)
    dims = (((1,), (1 if nt else 0,)), ((), ()))
    dot = partial(lax.dot_general, dimension_numbers=dims, preferred_element_type=F32)
    return dot(left[0], high) + (dot(left[0], low) + dot(left[1], high))


def kernel(
    grad_hbm, gate_hbm, spec_hbm, filt_hbm, wide_hbm, lanes_hbm, inner_hbm, lane_rows_hbm, picked_hbm,
    gi_out, gg_out, gf_out,
    grad, gate, spec, filt, wide, lanes, inner, lane_rows, picked,
    pre, mid, midt,
    x_out, x_in, y_out, y_in, c_out, c_in, i_out, i_in, d_out, d_in, e_out,
    prods, fsum, fpart, f_out, f_in, g_out, g_in, g_all, gf,
    load_sem, send_sem, recv_sem,
):
    me = lax.axis_index("ctx")
    group = lax.axis_index("ch")
    core = group % 2
    plane = group // 2
    other = group + 1 - 2 * core
    peers = [(me // 4 + dx) % 4 * 4 + (me + dz) % 4 for dx, dz in STEPS]

    def load(k, src, dst):
        copy = pltpu.make_async_copy(src, dst, load_sem.at[k])
        copy.start()
        return copy

    loads = [load(0, grad_hbm, grad), load(1, gate_hbm, gate)]

    barrier = pltpu.get_barrier_semaphore()
    for peer in peers:
        pl.semaphore_signal(barrier, inc=1, device_id={"ctx": peer}, device_id_type=MESH)
        pl.semaphore_signal(barrier, inc=1, device_id={"ctx": peer, "ch": other}, device_id_type=MESH)
    for step in range(1, 4):
        for side in range(2):
            there = 2 * ((plane + step) % 4) + side
            pl.semaphore_signal(barrier, inc=1, device_id={"ch": there}, device_id_type=MESH)
    pl.semaphore_signal(barrier, inc=1, device_id={"ch": other}, device_id_type=MESH)

    loads += [
        load(2, inner_hbm, inner),
        load(3, lane_rows_hbm, lane_rows),
        load(4, picked_hbm, picked),
        load(5, filt_hbm.at[:, plane], filt),
        load(6, spec_hbm, spec),
        load(7, lanes_hbm, lanes),
        load(8, wide_hbm, wide),
    ]

    def send_all(k, out, into):
        for peer in peers:
            pltpu.make_async_remote_copy(
                out.at[peer], into.at[me], send_sem.at[k], recv_sem.at[k],
                device_id={"ctx": peer}, device_id_type=MESH,
            ).start()
        into[me] = out[me]

    def send_piece(k, out, into, b, half):
        for peer in peers:
            pltpu.make_async_remote_copy(
                out.at[b, peer, half], into.at[b, me, half], send_sem.at[k], recv_sem.at[k],
                device_id={"ctx": peer}, device_id_type=MESH,
            ).start()

    def piece(ref, b, half):
        return ref.at[b, pl.ds(0, SHARDS - 1), half]

    def bulk(k, ref):
        return pltpu.make_async_remote_copy(
            ref, ref, send_sem.at[k], recv_sem.at[k], device_id={"ctx": (me + 1) % SHARDS}, device_id_type=MESH
        )

    def arrived(k, into):
        bulk(k, into.at[pl.ds(0, SHARDS - 1)]).wait_recv()

    def left(k, out):
        bulk(k, out.at[pl.ds(0, SHARDS - 1)]).wait_send()

    loads[0].wait()
    loads[1].wait()
    x_out[...] = (grad[...] * gate[...]).reshape(SHARDS, 32, LANES)

    pl.semaphore_wait(barrier, 2 * SHARDS - 1 + 6)
    send_all(0, x_out, x_in)

    for k in (2, 3, 4):
        loads[k].wait()
    lane_ids = lax.broadcasted_iota(jnp.int32, (WIDE, LANES), 1)
    for b in range(2):
        row = 2 * me + b
        for ri in range(2):
            column = jnp.sum(jnp.where(lane_ids == row + RADIX * ri, picked[...], 0.0), axis=1, keepdims=True)
            pre[b, ri] = jnp.broadcast_to(column, (WIDE, LANES))
        vr = lane_rows[0, pl.ds(row, 1), :]
        vi = lane_rows[1, pl.ds(row, 1), :]
        tr = inner[0] * vr - inner[1] * vi
        ti = inner[0] * vi + inner[1] * vr
        mid[b, 0] = tr
        mid[b, 1] = ti
        midt[b, 0] = tr.T * 0.5
        midt[b, 1] = ti.T * 0.5

    def spread(ref, b):
        return jnp.concatenate([ref[pl.ds(2 * s + b, LANES, stride=4), :] for s in range(2)], axis=1)

    loads[5].wait()
    loads[6].wait()
    for b in range(2):
        prods[b, 0, 0], prods[b, 0, 1] = spread(filt.at[0], b), spread(filt.at[1], b)
        for ch in range(2):
            prods[b, 1 + ch, 0], prods[b, 1 + ch, 1] = spread(spec.at[0, ch], b), spread(spec.at[1, ch], b)
    loads[7].wait()
    loads[8].wait()

    def inverse_rows(b, arrays):
        mr, mi = midt[b, 0], midt[b, 1]
        stacked = []
        for re, im in arrays:
            c = product(lanes[1], jnp.concatenate([re, im], axis=0))
            cr, ci = c[:LANES], c[LANES:]
            stacked.append(jnp.concatenate([cr * mr + ci * mi, ci * mr - cr * mi], axis=1))
        t = product(wide[1], jnp.concatenate(stacked, axis=0) if len(stacked) > 1 else stacked[0], nt=True)
        pr, pi = pre[b, 0], pre[b, 1]
        out = []
        for k in range(len(arrays)):
            sr = t[:WIDE, LANES * k : LANES * (k + 1)]
            si = t[WIDE:, LANES * k : LANES * (k + 1)]
            out.append((sr * pr + si * pi, si * pr - sr * pi))
        return out

    def put_row(out, b, arrays):
        for ch, both in enumerate(inverse_rows(b, arrays)):
            for ri in range(2):
                pieces = both[ri].reshape(SHARDS, 16, LANES)
                for half in range(2):
                    out[b, :, half, ri, ch] = pieces[:, 8 * half : 8 * half + 8]

    def conv_row(b):
        hr, hi = prods[b, 0, 0], prods[b, 0, 1]
        arrays = []
        for ch in range(2):
            ur, ui = prods[b, 1 + ch, 0], prods[b, 1 + ch, 1]
            arrays.append((ur * hr - ui * hi, ur * hi + ui * hr))
        put_row(c_out, b, arrays)

    def slab_forward(step, carry):
        ch, half = step // 2, step % 2
        xs = [x_in[j, pl.ds(16 * half + ch, 8, stride=2), :] for j in range(SHARDS)]
        ys = real_dft(xs + [None] * SHARDS)
        at = pl.ds(pl.multiple_of(8 * half, 8), 8)
        for r in range(RADIX):
            re, im = ys[min(r, RADIX - r)]
            if im is None:
                im = jnp.zeros_like(re)
            elif r > RADIX // 2:
                im = -im
            y_out[r % 2, r // 2, 0, ch, at, :] = re
            y_out[r % 2, r // 2, 1, ch, at, :] = im
        return carry

    def conv_step(step, carry):
        conv_row(step)

        @pl.when(step == 0)
        def _():
            send_piece(3, c_out, c_in, 0, 0)
            c_in[0, me] = c_out[0, me]
            arrived(0, x_in)
            lax.fori_loop(0, 4, slab_forward, 0)
            for turn in range(2):
                b = (1 - core + turn) % 2
                send_all(1 + turn, y_out.at[b], y_in.at[b])
            send_piece(16, c_out, c_in, 0, 1)

        return carry

    lax.fori_loop(0, 2, conv_step, 0)
    send_all(4, c_out.at[1], c_in.at[1])

    swap = pltpu.make_async_remote_copy(
        fsum.at[1 - core], fpart, send_sem.at[5], recv_sem.at[5], device_id={"ch": other}, device_id_type=MESH
    )

    def forward_row(turn):
        b = (1 - core + turn) % 2
        bulk(1 + turn, y_in.at[b, pl.ds(0, SHARDS - 1)]).wait_recv()
        pr = jnp.concatenate([pre[b, 0]] * 2, axis=1)
        pi = jnp.concatenate([pre[b, 1]] * 2, axis=1)
        yr = jnp.concatenate([y_in[b, :, 0, ch].reshape(WIDE, LANES) for ch in range(2)], axis=1)
        yi = jnp.concatenate([y_in[b, :, 1, ch].reshape(WIDE, LANES) for ch in range(2)], axis=1)
        a = product(wide[0], jnp.concatenate([yr * pr - yi * pi, yr * pi + yi * pr], axis=0))
        mr, mi = mid[b, 0], mid[b, 1]
        fr = fi = None
        for ch in range(2):
            ar = a[:WIDE, LANES * ch : LANES * (ch + 1)]
            ai = a[WIDE:, LANES * ch : LANES * (ch + 1)]
            g = product(lanes[0], jnp.concatenate([ar * mr - ai * mi, ar * mi + ai * mr], axis=1), nt=True)
            gr, gi = g[:LANES], g[LANES:]
            ur, ui = prods[b, 1 + ch, 0], prods[b, 1 + ch, 1]
            wr, wi = ur * gr + ui * gi, ur * gi - ui * gr
            fr, fi = (wr, wi) if ch == 0 else (fr + wr, fi + wi)
            hr, hi = prods[b, 0, 0], prods[b, 0, 1]
            prods[b, 1 + ch, 0], prods[b, 1 + ch, 1] = hr * gr + hi * gi, hr * gi - hi * gr
        fsum[b, 0], fsum[b, 1] = fr, fi

        return b

    def input_row(b):
        arrays = [(prods[b, 1 + ch, 0], prods[b, 1 + ch, 1]) for ch in range(2)]
        put_row(i_out, b, arrays)

    def filter_row():
        swap.wait_recv()
        ((re, im),) = inverse_rows(core, [(fsum[core, 0] + fpart[0], fsum[core, 1] + fpart[1])])
        f_out[:, 0] = re.reshape(2 * SHARDS, 8, LANES)
        f_out[:, 1] = im.reshape(2 * SHARDS, 8, LANES)
        for peer in peers + [me]:
            for side in range(2):
                if peer is me and side == 0:
                    continue
                there = other if side else group
                half = 1 - core if side else core
                pltpu.make_async_remote_copy(
                    f_out.at[2 * peer + half], f_in.at[2 * me + core], send_sem.at[6], recv_sem.at[6],
                    device_id={"ctx": peer, "ch": there}, device_id_type=MESH,
                ).start()
        f_in[2 * me + core] = f_out[2 * me + core]

    def row_turn(turn, carry):
        b = forward_row(turn)

        @pl.when(turn == 0)
        def _():
            swap.start()

        @pl.when(turn == 1)
        def _():
            filter_row()
            send_piece(7, i_out, i_in, 1 - core, 0)

        input_row(b)

        return carry

    lax.fori_loop(0, 2, row_turn, 0)
    send_piece(8, i_out, i_in, core, 0)
    i_in[0, me] = i_out[0, me]
    i_in[1, me] = i_out[1, me]

    def slab_back(row, put):
        ws = [None] * RADIX
        for r in range(RADIX // 2 + 1):
            q = (RADIX - r) % RADIX
            a = row(r, 0, 0) + row(q, 0, 0)
            c = row(r, 0, 1) + row(q, 0, 1)
            if q == r:
                ws[r] = (a, c)
                continue
            bb = row(r, 1, 0) - row(q, 1, 0)
            d = row(r, 1, 1) - row(q, 1, 1)
            ws[r] = (a - d, bb + c)
            ws[q] = (a + d, c - bb)
        for j, (re, im) in enumerate(back_dft(ws, first_half=True)):
            put(j, 0, re)
            put(j, 1, im)

    def conv_back(half, carry):
        def put(j, ch, value):
            d_out[j, pl.ds(16 * half + ch, 8, stride=2), :] = value

        slab_back(lambda r, ri, ch: c_in[r % 2, r // 2, half, ri, ch], put)
        return carry

    bulk(3, piece(c_in, 0, 0)).wait_recv()
    bulk(16, piece(c_in, 0, 1)).wait_recv()
    arrived(4, c_in.at[1])
    lax.fori_loop(0, 2, conv_back, 0)

    bulk(6, f_in.at[pl.ds(0, 2 * SHARDS - 1)]).wait_recv()
    ws = [(f_in[r, 0], f_in[r, 1]) for r in range(RADIX)]
    for j, (re, _) in enumerate(back_dft(ws, first_half=True)):
        g_out[j] = re + re
    send_all(10, g_out, g_in)
    send_piece(15, i_out, i_in, 1 - core, 1)
    send_piece(17, i_out, i_in, core, 1)
    send_all(9, d_out, d_in)

    share = pltpu.make_async_remote_copy(
        g_all.at[core], g_all.at[core], send_sem.at[14], recv_sem.at[14],
        device_id={"ch": other}, device_id_type=MESH,
    )

    def input_back(half, carry):
        bulk(7 + 8 * half, piece(i_in, 1 - core, half)).wait_recv()
        bulk(8 + 9 * half, piece(i_in, core, half)).wait_recv()

        def put(j, ch, value):
            e_out[half, j, pl.ds(ch, 8, stride=2), :] = value

        slab_back(lambda r, ri, ch: i_in[r % 2, r // 2, half, ri, ch], put)
        for peer in peers:
            pltpu.make_async_remote_copy(
                e_out.at[half, peer], gi_out.at[me, half], send_sem.at[11 + half], recv_sem.at[11 + half],
                device_id={"ctx": peer}, device_id_type=MESH,
            ).start()
        own = pltpu.make_async_copy(e_out.at[half, me], gi_out.at[me, half], load_sem.at[half])
        own.start()

        @pl.when(half == 0)
        def _():
            arrived(10, g_in)
            for step in range(1, 4):
                pltpu.make_async_remote_copy(
                    g_in, g_all.at[core, plane], send_sem.at[13], recv_sem.at[13],
                    device_id={"ch": 2 * ((plane + step) % 4) + core}, device_id_type=MESH,
                ).start()
            g_all[core, plane] = g_in[...]

        @pl.when(half == 1)
        def _():
            bulk(13, g_all.at[core, pl.ds(0, 3)]).wait_recv()
            share.start()

        own.wait()
        return carry

    lax.fori_loop(0, 2, input_back, 0)

    arrived(9, d_in)
    gate[...] = grad[...] * d_in[...].reshape(512, LANES)
    store_gg = load(2, gate, gg_out)
    share.wait_recv()
    for f in range(FILTERS):
        for c in range(2):
            for q in range(SHARDS):
                gf[pl.ds(64 * q + 32 * c + f, 8, stride=4), :] = g_all[c, f, q]
    store_gf = load(3, gf, gf_out)
    bulk(11, e_out.at[0, pl.ds(0, SHARDS - 1)]).wait_recv()
    bulk(12, e_out.at[1, pl.ds(0, SHARDS - 1)]).wait_recv()

    left(0, x_out)
    for turn in range(2):
        left(1 + turn, y_out.at[turn])
        bulk(3 + 13 * turn, piece(c_out, 0, turn)).wait_send()
        bulk(7 + 8 * turn, piece(i_out, 1 - core, turn)).wait_send()
        bulk(8 + 9 * turn, piece(i_out, core, turn)).wait_send()
        left(11 + turn, e_out.at[turn])
    swap.wait_send()
    bulk(6, f_out.at[pl.ds(0, 2 * SHARDS - 1)]).wait_send()
    left(4, c_out.at[1])
    left(9, d_out)
    left(10, g_out)
    bulk(13, g_all.at[core, pl.ds(0, 3)]).wait_send()
    share.wait_send()
    store_gg.wait()
    store_gf.wait()


def store_results(*refs):
    ins, outs, sem = refs[:3], refs[3:6], refs[6]
    copies = [pltpu.make_async_copy(src, dst, sem.at[k]) for k, (src, dst) in enumerate(zip(ins, outs))]
    for copy in copies:
        copy.start()
    for copy in copies:
        copy.wait()


def per_device(grad_out, gate_in, input_spectrum, filter_spectrum):
    def tiled(x):
        lead = x.shape[:-2]
        pieces = x.reshape(*lead, x.shape[-2], WIDE, LANES)
        return jnp.swapaxes(pieces, -3, -2).reshape(*lead, WIDE * x.shape[-2], LANES)

    def untiled(x, rows):
        return jnp.swapaxes(x.reshape(WIDE, rows, LANES), 0, 1).reshape(rows, COLS)

    consts = tables()
    operands = (tiled(grad_out), tiled(gate_in), tiled(input_spectrum), tiled(filter_spectrum), *consts)
    slab = lambda *dims: pltpu.VMEM((SHARDS, *dims, LANES), F32)
    wave = pltpu.VMEM((2, SHARDS, 2, 2, 16, LANES), F32)
    half_wave = pltpu.VMEM((2, SHARDS, 2, 2, 2, 8, LANES), F32)
    scratch = [
        pltpu.VMEM((512, LANES), F32),
        pltpu.VMEM((512, LANES), F32),
        pltpu.VMEM((2, 2, 512, LANES), F32),
        pltpu.VMEM((2, 512, LANES), F32),
        *[pltpu.VMEM(c.shape, c.dtype) for c in consts],
        pltpu.VMEM((2, 2, WIDE, LANES), F32),
        pltpu.VMEM((2, 2, WIDE, LANES), F32),
        pltpu.VMEM((2, 2, LANES, WIDE), F32),
        slab(32),
        slab(32),
        wave,
        wave,
        half_wave,
        half_wave,
        half_wave,
        half_wave,
        slab(32),
        slab(32),
        pltpu.VMEM((2, SHARDS, 16, LANES), F32),
        pltpu.VMEM((2, 3, 2, LANES, WIDE), F32),
        pltpu.VMEM((2, 2, LANES, WIDE), F32),
        pltpu.VMEM((2, LANES, WIDE), F32),
        pltpu.VMEM((2 * SHARDS, 2, 8, LANES), F32),
        pltpu.VMEM((2 * SHARDS, 2, 8, LANES), F32),
        slab(8),
        slab(8),
        pltpu.VMEM((2, 4, SHARDS, 8, LANES), F32),
        pltpu.VMEM((1024, LANES), F32),
        pltpu.SemaphoreType.DMA((9,)),
        pltpu.SemaphoreType.DMA((18,)),
        pltpu.SemaphoreType.DMA((18,)),
    ]
    in_hbm = pl.BlockSpec(memory_space=pltpu.HBM)
    anywhere = pl.BlockSpec(memory_space=pl.ANY)
    results = [
        jax.ShapeDtypeStruct((SHARDS, 2, 16, LANES), F32),
        jax.ShapeDtypeStruct((512, LANES), F32),
        jax.ShapeDtypeStruct((1024, LANES), F32),
    ]
    found = pl.pallas_call(
        kernel,
        out_shape=results,
        in_specs=[in_hbm] * len(operands),
        out_specs=[anywhere] * 3,
        scratch_shapes=scratch,
        compiler_params=pltpu.CompilerParams(
            collective_id=0, has_side_effects=True, vmem_limit_bytes=40 * 2**20
        ),
        name="gated_conv_back",
    )(*[pltpu.with_memory_space_constraint(x, pltpu.HBM) for x in operands])
    grad_input, grad_gate, grad_filter = pl.pallas_call(
        store_results,
        out_shape=results,
        in_specs=[anywhere] * 3,
        out_specs=[in_hbm] * 3,
        scratch_shapes=[pltpu.SemaphoreType.DMA((3,))],
        compiler_params=pltpu.CompilerParams(vmem_limit_bytes=2**20),
        name="store_results",
    )(*found)
    return (
        untiled(grad_input.reshape(512, LANES), 2),
        untiled(grad_gate, 2),
        untiled(grad_filter, 4),
    )


def solution(mesh):
    return jax.shard_map(
        per_device,
        mesh=mesh,
        in_specs=(
            P("ch", "ctx"),
            P("ch", "ctx"),
            P(None, "ch", "ctx", None),
            P(None, None, "ctx", None),
        ),
        out_specs=(P("ch", "ctx"), P("ch", "ctx"), P(None, "ctx")),
        check_vma=False,
    )
```

```python
from functools import partial
import math

import jax
import jax.numpy as jnp
import numpy as np
from jax import lax
from jax.experimental import pallas as pl
from jax.experimental.pallas import tpu as pltpu
from jax.sharding import PartitionSpec as P

CHANNELS = 16
FILTERS = 4
RADIX = 32
COLS = 32768
TOTAL = RADIX * COLS
SHARDS = 16
WIDE = 256
LANES = 128
MESH = pl.DeviceIdType.MESH
STEPS = (
    (2, 2), (2, 1), (1, 2), (2, 3), (3, 2), (2, 0), (0, 2),
    (1, 1), (3, 3), (1, 3), (3, 1), (1, 0), (0, 1), (3, 0), (0, 3),
)
F32 = jnp.float32
BF16 = jnp.bfloat16


def real_form(matrix):
    return np.block([[matrix.real, -matrix.imag], [matrix.imag, matrix.real]])


def halves(matrix):
    whole = matrix.astype(np.float32)
    high = whole.astype(jnp.bfloat16)
    low = (matrix - high.astype(np.float64)).astype(np.float32).astype(jnp.bfloat16)
    return np.stack([high, low])


def tables():
    def unit(counts, modulus):
        return np.exp(-2j * np.pi * (counts % modulus) / modulus)

    wide = np.arange(WIDE)
    lanes = np.arange(LANES)
    rows = np.arange(RADIX)
    dft_wide = unit(wide[:, None] * wide[None, :], WIDE)
    dft_lanes = unit(lanes[:, None] * lanes[None, :], LANES)
    inner = unit(wide[:, None] * lanes[None, :], COLS) * 2.0**-10
    lane_rows = unit(rows[:, None] * lanes[None, :], TOTAL)
    wide_rows = unit(wide[:, None] * rows[None, :], TOTAL // LANES)
    picked = np.concatenate([wide_rows.real, wide_rows.imag, np.zeros((WIDE, LANES - 2 * RADIX))], axis=1)
    return (
        np.stack([halves(real_form(dft_wide)), halves(real_form(dft_wide.conj()))]),
        np.stack([halves(real_form(dft_lanes)), halves(real_form(dft_lanes.conj()))]),
        np.stack([inner.real, inner.imag]).astype(np.float32),
        np.stack([lane_rows.real, lane_rows.imag]).astype(np.float32),
        picked.astype(np.float32),
    )


def times_unit(value, turn):
    re, im = value
    turn = turn % 1.0
    if turn == 0.0:
        return re, im
    if turn == 0.5:
        return negated(re), negated(im)
    if turn == 0.25:
        return negated(im), re
    if turn == 0.75:
        return im, negated(re)
    c, s = math.cos(2 * math.pi * turn), math.sin(2 * math.pi * turn)
    if im is None:
        return re * c, re * s
    if re is None:
        return im * (-s), im * c
    if turn in (0.125, 0.375, 0.625, 0.875):
        h = math.sqrt(0.5)
        if turn == 0.125:
            return (re - im) * h, (re + im) * h
        if turn == 0.375:
            return (re + im) * (-h), (re - im) * h
        if turn == 0.625:
            return (im - re) * h, (re + im) * (-h)
        return (re + im) * h, (im - re) * h
    return re * c - im * s, re * s + im * c


def negated(x):
    return None if x is None else -x


def plus(a, b):
    if a is None:
        return b
    return a if b is None else a + b


def minus(a, b):
    if b is None:
        return a
    return -b if a is None else a - b


def real_dft(xs):
    n = len(xs)
    if n == 1:
        return [(xs[0], None)]
    even, odd = real_dft(xs[0::2]), real_dft(xs[1::2])
    if n == 2:
        a, b = even[0][0], odd[0][0]
        return [(plus(a, b), None), (minus(a, b), None)]
    out = [None] * (n // 2 + 1)
    for k in range(n // 4 + 1):
        e, t = even[k], times_unit(odd[k], -k / n)
        out[k] = (plus(e[0], t[0]), plus(e[1], t[1]))
        if n // 2 - k != k:
            out[n // 2 - k] = (minus(e[0], t[0]), minus(t[1], e[1]))
    return out


def back_dft(xs, first_half=False):
    n = len(xs)
    if n == 1:
        return list(xs)
    even, odd = back_dft(xs[0::2]), back_dft(xs[1::2])
    upper, lower = [], []
    for k in range(n // 2):
        e, t = even[k], times_unit(odd[k], k / n)
        upper.append((e[0] + t[0], e[1] + t[1]))
        if not first_half:
            lower.append((e[0] - t[0], e[1] - t[1]))
    return upper + lower


def parts(x):
    high = x.astype(BF16)
    return high, (x - high.astype(F32)).astype(BF16)


def product(left, x, nt=False):
    high, low = parts(x)
    dims = (((1,), (1 if nt else 0,)), ((), ()))
    dot = partial(lax.dot_general, dimension_numbers=dims, preferred_element_type=F32)
    return dot(left[0], high) + (dot(left[0], low) + dot(left[1], high))


def kernel(
    grad_hbm, gate_hbm, spec_hbm, filt_hbm, wide_hbm, lanes_hbm, inner_hbm, lane_rows_hbm, picked_hbm,
    gi_out, gg_out, gf_out,
    grad, gate, spec, filt, wide, lanes, inner, lane_rows, picked,
    pre, mid, midt,
    x_out, x_in, y_out, y_in, c_out, c_in, i_out, i_in, d_out, d_in, e_out,
    prods, fsum, fpart, f_out, f_in, g_out, g_in, g_all, gf,
    load_sem, send_sem, recv_sem,
):
    me = lax.axis_index("ctx")
    group = lax.axis_index("ch")
    core = group % 2
    plane = group // 2
    other = group + 1 - 2 * core
    peers = [(me // 4 + dx) % 4 * 4 + (me + dz) % 4 for dx, dz in STEPS]

    def load(k, src, dst):
        copy = pltpu.make_async_copy(src, dst, load_sem.at[k])
        copy.start()
        return copy

    loads = [load(0, grad_hbm, grad), load(1, gate_hbm, gate)]

    barrier = pltpu.get_barrier_semaphore()
    for peer in peers:
        pl.semaphore_signal(barrier, inc=1, device_id={"ctx": peer}, device_id_type=MESH)
        pl.semaphore_signal(barrier, inc=1, device_id={"ctx": peer, "ch": other}, device_id_type=MESH)
    for step in range(1, 4):
        for side in range(2):
            there = 2 * ((plane + step) % 4) + side
            pl.semaphore_signal(barrier, inc=1, device_id={"ch": there}, device_id_type=MESH)
    pl.semaphore_signal(barrier, inc=1, device_id={"ch": other}, device_id_type=MESH)

    loads += [
        load(2, inner_hbm, inner),
        load(3, lane_rows_hbm, lane_rows),
        load(4, picked_hbm, picked),
        load(5, filt_hbm.at[:, plane], filt),
        load(6, spec_hbm, spec),
        load(7, lanes_hbm, lanes),
        load(8, wide_hbm, wide),
    ]

    def send_all(k, out, into):
        for peer in peers:
            pltpu.make_async_remote_copy(
                out.at[peer], into.at[me], send_sem.at[k], recv_sem.at[k],
                device_id={"ctx": peer}, device_id_type=MESH,
            ).start()
        into[me] = out[me]

    def send_piece(k, out, into, b, half):
        for peer in peers:
            pltpu.make_async_remote_copy(
                out.at[b, peer, half], into.at[b, me, half], send_sem.at[k], recv_sem.at[k],
                device_id={"ctx": peer}, device_id_type=MESH,
            ).start()

    def piece(ref, b, half):
        return ref.at[b, pl.ds(0, SHARDS - 1), half]

    def bulk(k, ref):
        return pltpu.make_async_remote_copy(
            ref, ref, send_sem.at[k], recv_sem.at[k], device_id={"ctx": (me + 1) % SHARDS}, device_id_type=MESH
        )

    def arrived(k, into):
        bulk(k, into.at[pl.ds(0, SHARDS - 1)]).wait_recv()

    def left(k, out):
        bulk(k, out.at[pl.ds(0, SHARDS - 1)]).wait_send()

    loads[0].wait()
    loads[1].wait()
    x_out[...] = (grad[...] * gate[...]).reshape(SHARDS, 32, LANES)

    pl.semaphore_wait(barrier, 2 * SHARDS - 1 + 6)
    send_all(0, x_out, x_in)

    for k in (2, 3, 4):
        loads[k].wait()
    lane_ids = lax.broadcasted_iota(jnp.int32, (WIDE, LANES), 1)
    for b in range(2):
        row = 2 * me + b
        for ri in range(2):
            column = jnp.sum(jnp.where(lane_ids == row + RADIX * ri, picked[...], 0.0), axis=1, keepdims=True)
            pre[b, ri] = jnp.broadcast_to(column, (WIDE, LANES))
        vr = lane_rows[0, pl.ds(row, 1), :]
        vi = lane_rows[1, pl.ds(row, 1), :]
        tr = inner[0] * vr - inner[1] * vi
        ti = inner[0] * vi + inner[1] * vr
        mid[b, 0] = tr
        mid[b, 1] = ti
        midt[b, 0] = tr.T * 0.5
        midt[b, 1] = ti.T * 0.5

    def spread(ref, b):
        return jnp.concatenate([ref[pl.ds(2 * s + b, LANES, stride=4), :] for s in range(2)], axis=1)

    loads[5].wait()
    loads[6].wait()
    for b in range(2):
        prods[b, 0, 0], prods[b, 0, 1] = spread(filt.at[0], b), spread(filt.at[1], b)
        for ch in range(2):
            prods[b, 1 + ch, 0], prods[b, 1 + ch, 1] = spread(spec.at[0, ch], b), spread(spec.at[1, ch], b)
    loads[7].wait()
    loads[8].wait()

    def inverse_rows(b, arrays):
        mr, mi = midt[b, 0], midt[b, 1]
        stacked = []
        for re, im in arrays:
            c = product(lanes[1], jnp.concatenate([re, im], axis=0))
            cr, ci = c[:LANES], c[LANES:]
            stacked.append(jnp.concatenate([cr * mr + ci * mi, ci * mr - cr * mi], axis=1))
        t = product(wide[1], jnp.concatenate(stacked, axis=0) if len(stacked) > 1 else stacked[0], nt=True)
        pr, pi = pre[b, 0], pre[b, 1]
        out = []
        for k in range(len(arrays)):
            sr = t[:WIDE, LANES * k : LANES * (k + 1)]
            si = t[WIDE:, LANES * k : LANES * (k + 1)]
            out.append((sr * pr + si * pi, si * pr - sr * pi))
        return out

    def put_row(out, b, arrays):
        for ch, both in enumerate(inverse_rows(b, arrays)):
            for ri in range(2):
                pieces = both[ri].reshape(SHARDS, 16, LANES)
                for half in range(2):
                    out[b, :, half, ri, ch] = pieces[:, 8 * half : 8 * half + 8]

    def conv_row(b):
        hr, hi = prods[b, 0, 0], prods[b, 0, 1]
        arrays = []
        for ch in range(2):
            ur, ui = prods[b, 1 + ch, 0], prods[b, 1 + ch, 1]
            arrays.append((ur * hr - ui * hi, ur * hi + ui * hr))
        put_row(c_out, b, arrays)

    def slab_forward(step, carry):
        ch, half = step // 2, step % 2
        xs = [x_in[j, pl.ds(16 * half + ch, 8, stride=2), :] for j in range(SHARDS)]
        ys = real_dft(xs + [None] * SHARDS)
        at = pl.ds(pl.multiple_of(8 * half, 8), 8)
        for r in range(RADIX):
            re, im = ys[min(r, RADIX - r)]
            if im is None:
                im = jnp.zeros_like(re)
            elif r > RADIX // 2:
                im = -im
            y_out[r % 2, r // 2, 0, ch, at, :] = re
            y_out[r % 2, r // 2, 1, ch, at, :] = im
        return carry

    def conv_step(step, carry):
        conv_row(step)

        @pl.when(step == 0)
        def _():
            send_piece(3, c_out, c_in, 0, 0)
            c_in[0, me] = c_out[0, me]
            arrived(0, x_in)
            lax.fori_loop(0, 4, slab_forward, 0)
            for turn in range(2):
                b = (1 - core + turn) % 2
                send_all(1 + turn, y_out.at[b], y_in.at[b])
            send_piece(16, c_out, c_in, 0, 1)

        return carry

    lax.fori_loop(0, 2, conv_step, 0)
    send_all(4, c_out.at[1], c_in.at[1])

    swap = pltpu.make_async_remote_copy(
        fsum.at[1 - core], fpart, send_sem.at[5], recv_sem.at[5], device_id={"ch": other}, device_id_type=MESH
    )

    def forward_row(turn):
        b = (1 - core + turn) % 2
        bulk(1 + turn, y_in.at[b, pl.ds(0, SHARDS - 1)]).wait_recv()
        pr = jnp.concatenate([pre[b, 0]] * 2, axis=1)
        pi = jnp.concatenate([pre[b, 1]] * 2, axis=1)
        yr = jnp.concatenate([y_in[b, :, 0, ch].reshape(WIDE, LANES) for ch in range(2)], axis=1)
        yi = jnp.concatenate([y_in[b, :, 1, ch].reshape(WIDE, LANES) for ch in range(2)], axis=1)
        a = product(wide[0], jnp.concatenate([yr * pr - yi * pi, yr * pi + yi * pr], axis=0))
        mr, mi = mid[b, 0], mid[b, 1]
        fr = fi = None
        for ch in range(2):
            ar = a[:WIDE, LANES * ch : LANES * (ch + 1)]
            ai = a[WIDE:, LANES * ch : LANES * (ch + 1)]
            g = product(lanes[0], jnp.concatenate([ar * mr - ai * mi, ar * mi + ai * mr], axis=1), nt=True)
            gr, gi = g[:LANES], g[LANES:]
            ur, ui = prods[b, 1 + ch, 0], prods[b, 1 + ch, 1]
            wr, wi = ur * gr + ui * gi, ur * gi - ui * gr
            fr, fi = (wr, wi) if ch == 0 else (fr + wr, fi + wi)
            hr, hi = prods[b, 0, 0], prods[b, 0, 1]
            prods[b, 1 + ch, 0], prods[b, 1 + ch, 1] = hr * gr + hi * gi, hr * gi - hi * gr
        fsum[b, 0], fsum[b, 1] = fr, fi

        return b

    def input_row(b):
        arrays = [(prods[b, 1 + ch, 0], prods[b, 1 + ch, 1]) for ch in range(2)]
        put_row(i_out, b, arrays)

    def filter_row():
        swap.wait_recv()
        ((re, im),) = inverse_rows(core, [(fsum[core, 0] + fpart[0], fsum[core, 1] + fpart[1])])
        f_out[:, 0] = re.reshape(2 * SHARDS, 8, LANES)
        f_out[:, 1] = im.reshape(2 * SHARDS, 8, LANES)
        for peer in peers + [me]:
            for side in range(2):
                if peer is me and side == 0:
                    continue
                there = other if side else group
                half = 1 - core if side else core
                pltpu.make_async_remote_copy(
                    f_out.at[2 * peer + half], f_in.at[2 * me + core], send_sem.at[6], recv_sem.at[6],
                    device_id={"ctx": peer, "ch": there}, device_id_type=MESH,
                ).start()
        f_in[2 * me + core] = f_out[2 * me + core]

    def row_turn(turn, carry):
        b = forward_row(turn)

        @pl.when(turn == 0)
        def _():
            swap.start()

        @pl.when(turn == 1)
        def _():
            filter_row()
            send_piece(7, i_out, i_in, 1 - core, 0)

        input_row(b)

        return carry

    lax.fori_loop(0, 2, row_turn, 0)
    send_piece(8, i_out, i_in, core, 0)
    i_in[0, me] = i_out[0, me]
    i_in[1, me] = i_out[1, me]

    def slab_back(row, put):
        ws = [None] * RADIX
        for r in range(RADIX // 2 + 1):
            q = (RADIX - r) % RADIX
            a = row(r, 0, 0) + row(q, 0, 0)
            c = row(r, 0, 1) + row(q, 0, 1)
            if q == r:
                ws[r] = (a, c)
                continue
            bb = row(r, 1, 0) - row(q, 1, 0)
            d = row(r, 1, 1) - row(q, 1, 1)
            ws[r] = (a - d, bb + c)
            ws[q] = (a + d, c - bb)
        for j, (re, im) in enumerate(back_dft(ws, first_half=True)):
            put(j, 0, re)
            put(j, 1, im)

    def conv_back(half, carry):
        def put(j, ch, value):
            d_out[j, pl.ds(16 * half + ch, 8, stride=2), :] = value

        slab_back(lambda r, ri, ch: c_in[r % 2, r // 2, half, ri, ch], put)
        return carry

    bulk(3, piece(c_in, 0, 0)).wait_recv()
    bulk(16, piece(c_in, 0, 1)).wait_recv()
    arrived(4, c_in.at[1])
    lax.fori_loop(0, 2, conv_back, 0)

    bulk(6, f_in.at[pl.ds(0, 2 * SHARDS - 1)]).wait_recv()
    ws = [(f_in[r, 0], f_in[r, 1]) for r in range(RADIX)]
    for j, (re, _) in enumerate(back_dft(ws, first_half=True)):
        g_out[j] = re + re
    send_all(10, g_out, g_in)
    send_piece(15, i_out, i_in, 1 - core, 1)
    send_piece(17, i_out, i_in, core, 1)
    send_all(9, d_out, d_in)

    share = pltpu.make_async_remote_copy(
        g_all.at[core], g_all.at[core], send_sem.at[14], recv_sem.at[14],
        device_id={"ch": other}, device_id_type=MESH,
    )

    def input_back(half, carry):
        bulk(7 + 8 * half, piece(i_in, 1 - core, half)).wait_recv()
        bulk(8 + 9 * half, piece(i_in, core, half)).wait_recv()

        def put(j, ch, value):
            e_out[half, j, pl.ds(ch, 8, stride=2), :] = value

        slab_back(lambda r, ri, ch: i_in[r % 2, r // 2, half, ri, ch], put)
        for peer in peers:
            pltpu.make_async_remote_copy(
                e_out.at[half, peer], gi_out.at[me, half], send_sem.at[11 + half], recv_sem.at[11 + half],
                device_id={"ctx": peer}, device_id_type=MESH,
            ).start()
        own = pltpu.make_async_copy(e_out.at[half, me], gi_out.at[me, half], load_sem.at[half])
        own.start()

        @pl.when(half == 0)
        def _():
            arrived(10, g_in)
            for step in range(1, 4):
                pltpu.make_async_remote_copy(
                    g_in, g_all.at[core, plane], send_sem.at[13], recv_sem.at[13],
                    device_id={"ch": 2 * ((plane + step) % 4) + core}, device_id_type=MESH,
                ).start()
            g_all[core, plane] = g_in[...]

        @pl.when(half == 1)
        def _():
            bulk(13, g_all.at[core, pl.ds(0, 3)]).wait_recv()
            share.start()

        own.wait()
        return carry

    lax.fori_loop(0, 2, input_back, 0)

    arrived(9, d_in)
    gate[...] = grad[...] * d_in[...].reshape(512, LANES)
    store_gg = load(2, gate, gg_out)
    share.wait_recv()
    for f in range(FILTERS):
        for c in range(2):
            for q in range(SHARDS):
                gf[pl.ds(64 * q + 32 * c + f, 8, stride=4), :] = g_all[c, f, q]
    store_gf = load(3, gf, gf_out)
    bulk(11, e_out.at[0, pl.ds(0, SHARDS - 1)]).wait_recv()
    bulk(12, e_out.at[1, pl.ds(0, SHARDS - 1)]).wait_recv()

    left(0, x_out)
    for turn in range(2):
        left(1 + turn, y_out.at[turn])
        bulk(3 + 13 * turn, piece(c_out, 0, turn)).wait_send()
        bulk(7 + 8 * turn, piece(i_out, 1 - core, turn)).wait_send()
        bulk(8 + 9 * turn, piece(i_out, core, turn)).wait_send()
        left(11 + turn, e_out.at[turn])
    swap.wait_send()
    bulk(6, f_out.at[pl.ds(0, 2 * SHARDS - 1)]).wait_send()
    left(4, c_out.at[1])
    left(9, d_out)
    left(10, g_out)
    bulk(13, g_all.at[core, pl.ds(0, 3)]).wait_send()
    share.wait_send()
    store_gg.wait()
    store_gf.wait()


def store_results(*refs):
    ins, outs, sem = refs[:3], refs[3:6], refs[6]
    copies = []
    for src, dst in zip(ins, outs):
        step = src.shape[0] // 4
        for k in range(4):
            rows = pl.ds(k * step, step)
            copies.append(pltpu.make_async_copy(src.at[rows], dst.at[rows], sem.at[len(copies)]))
    for copy in copies:
        copy.start()
    for copy in copies:
        copy.wait()


def per_device(grad_out, gate_in, input_spectrum, filter_spectrum):
    def tiled(x):
        lead = x.shape[:-2]
        pieces = x.reshape(*lead, x.shape[-2], WIDE, LANES)
        return jnp.swapaxes(pieces, -3, -2).reshape(*lead, WIDE * x.shape[-2], LANES)

    def untiled(x, rows):
        return jnp.swapaxes(x.reshape(WIDE, rows, LANES), 0, 1).reshape(rows, COLS)

    consts = tables()
    operands = (tiled(grad_out), tiled(gate_in), tiled(input_spectrum), tiled(filter_spectrum), *consts)
    slab = lambda *dims: pltpu.VMEM((SHARDS, *dims, LANES), F32)
    wave = pltpu.VMEM((2, SHARDS, 2, 2, 16, LANES), F32)
    half_wave = pltpu.VMEM((2, SHARDS, 2, 2, 2, 8, LANES), F32)
    scratch = [
        pltpu.VMEM((512, LANES), F32),
        pltpu.VMEM((512, LANES), F32),
        pltpu.VMEM((2, 2, 512, LANES), F32),
        pltpu.VMEM((2, 512, LANES), F32),
        *[pltpu.VMEM(c.shape, c.dtype) for c in consts],
        pltpu.VMEM((2, 2, WIDE, LANES), F32),
        pltpu.VMEM((2, 2, WIDE, LANES), F32),
        pltpu.VMEM((2, 2, LANES, WIDE), F32),
        slab(32),
        slab(32),
        wave,
        wave,
        half_wave,
        half_wave,
        half_wave,
        half_wave,
        slab(32),
        slab(32),
        pltpu.VMEM((2, SHARDS, 16, LANES), F32),
        pltpu.VMEM((2, 3, 2, LANES, WIDE), F32),
        pltpu.VMEM((2, 2, LANES, WIDE), F32),
        pltpu.VMEM((2, LANES, WIDE), F32),
        pltpu.VMEM((2 * SHARDS, 2, 8, LANES), F32),
        pltpu.VMEM((2 * SHARDS, 2, 8, LANES), F32),
        slab(8),
        slab(8),
        pltpu.VMEM((2, 4, SHARDS, 8, LANES), F32),
        pltpu.VMEM((1024, LANES), F32),
        pltpu.SemaphoreType.DMA((9,)),
        pltpu.SemaphoreType.DMA((18,)),
        pltpu.SemaphoreType.DMA((18,)),
    ]
    in_hbm = pl.BlockSpec(memory_space=pltpu.HBM)
    anywhere = pl.BlockSpec(memory_space=pl.ANY)
    results = [
        jax.ShapeDtypeStruct((SHARDS, 2, 16, LANES), F32),
        jax.ShapeDtypeStruct((512, LANES), F32),
        jax.ShapeDtypeStruct((1024, LANES), F32),
    ]
    found = pl.pallas_call(
        kernel,
        out_shape=results,
        in_specs=[in_hbm] * len(operands),
        out_specs=[anywhere] * 3,
        scratch_shapes=scratch,
        compiler_params=pltpu.CompilerParams(
            collective_id=0, has_side_effects=True, vmem_limit_bytes=40 * 2**20
        ),
        name="gated_conv_back",
    )(*[pltpu.with_memory_space_constraint(x, pltpu.HBM) for x in operands])
    grad_input, grad_gate, grad_filter = pl.pallas_call(
        store_results,
        out_shape=results,
        in_specs=[anywhere] * 3,
        out_specs=[in_hbm] * 3,
        scratch_shapes=[pltpu.SemaphoreType.DMA((12,))],
        compiler_params=pltpu.CompilerParams(vmem_limit_bytes=2**20),
        name="store_results",
    )(*found)
    return (
        untiled(grad_input.reshape(512, LANES), 2),
        untiled(grad_gate, 2),
        untiled(grad_filter, 4),
    )


def solution(mesh):
    return jax.shard_map(
        per_device,
        mesh=mesh,
        in_specs=(
            P("ch", "ctx"),
            P("ch", "ctx"),
            P(None, "ch", "ctx", None),
            P(None, None, "ctx", None),
        ),
        out_specs=(P("ch", "ctx"), P("ch", "ctx"), P(None, "ctx")),
        check_vma=False,
    )
```
